32 devices in a mesh: ctx: 8 (over z, x), fsdp: 4 (over y, core).
Axes of the slice: x: 2, y: 2, z: 4, core: 2. Of those that a mesh axis runs over, the one named last changes fastest.
Arguments:
- query_in: bfloat16 [4096, 4096], P('ctx', 'fsdp'), may hold values from -6 to 6
- key_in: bfloat16 [4096, 4096], P('ctx', 'fsdp'), may hold values from -6 to 6
- value_in: bfloat16 [4096, 4096], P('ctx', 'fsdp'), may hold values from -6 to 6
- residues: float32 [16, 256], P(None, 'fsdp'), may hold values from -1.5 to 1.5
- decay_rate: float32 [16, 256], P(None, 'fsdp'), may hold values from 6.1035156e-05 to 0.1
- short_filter: float32 [3, 3, 4096], P(None, None, 'fsdp'), may hold values from -3 to 3
- skip_gain: float32 [1, 4096], P(None, 'fsdp'), may hold values from -3 to 3
Outputs:
- mixed_out: bfloat16 [4096, 4096], P('ctx', 'fsdp')
The draws below stay inside these ranges and needn't reach their ends.
All inputs are finite; a program needn't handle non-finite values.
Results may differ from the reference program's by a relative error of at most 0.001.
Values may be sent and summed in bfloat16 or wider, within the bound.
No kernel may reach another device: no remote copies, remote signals or barrier semaphores. Data moves between devices by JAX's collectives and lax.ppermute only.
A program may use at most 320 MiB of HBM per device.

```python
import jax
import jax.numpy as jnp
from jax import lax

D = 4096
FILTERS = 256
MODES = 16
SHORT = 3
SPAN = 512
GS = 16
TOTAL = 4096


def draw_decay_rate(key, part):
    first, second = jax.random.split(jax.random.fold_in(key, 17), 2)
    share = 0.5
    slow = jax.random.uniform(first, (MODES, FILTERS), jnp.float32) < share
    ratio = jax.random.uniform(second, (MODES, FILTERS), jnp.float32)
    low_slow = 0.25 / TOTAL
    high_slow = 2.0 / TOTAL
    slow_rate = jnp.exp(jnp.log(low_slow) + ratio * jnp.log(high_slow / low_slow))
    fast_rate = jnp.exp(jnp.log(high_slow) + ratio * jnp.log(0.1 / high_slow))
    return jnp.where(slow, slow_rate, fast_rate).astype(jnp.float32)


def block_levels(rng, dims, shards, smallest, top_value):
    def one(dim, shards_of):
        heights = jax.random.uniform(jax.random.fold_in(jax.random.fold_in(rng, 6), dim), (shards_of,), jnp.float32, smallest / len(shards), top_value / len(shards))
        return jnp.repeat(jnp.exp(heights), dims[dim] // shards_of).reshape((-1,) + (1,) * (len(dims) - dim - 1))

    factor_of = one(*shards[0])
    for cut in shards[1:]:
        factor_of = factor_of * one(*cut)
    return factor_of


def gaussian(own_key, extent, scale, most, shards=(), dtype=jnp.bfloat16):
    result = scale * jax.random.normal(own_key, extent, jnp.float32)
    if shards:
        result = result * block_levels(own_key, extent, shards, -0.22, 0.18)
    return jnp.clip(result, -most, most).astype(dtype)


def setup_inputs(seed: int = 0) -> dict:
    splits = jax.random.split(jax.random.key(seed), 8)
    query_in = gaussian(splits[0], (TOTAL, D), 1.0, 6.0, ((0, 8), (1, 4)))
    key_in = gaussian(splits[1], (TOTAL, D), 1.0, 6.0, ((0, 8), (1, 4)))
    value_in = gaussian(splits[2], (TOTAL, D), 1.0, 6.0, ((0, 8), (1, 4)))
    residues = gaussian(splits[3], (MODES, FILTERS), MODES ** -0.5, 1.5, ((1, 4),), jnp.float32)
    decay_rate = draw_decay_rate(jax.random.fold_in(splits[7], 71), 0)
    short_filter = gaussian(splits[5], (3, SHORT, D), 0.5, 3.0, ((2, 4),), jnp.float32)
    skip_gain = gaussian(splits[6], (1, D), 0.5, 3.0, ((1, 4),), jnp.float32)
    return {"query_in": query_in, "key_in": key_in, "value_in": value_in, "residues": residues, "decay_rate": decay_rate, "short_filter": short_filter, "skip_gain": skip_gain}


def filter_taps(residues, decay_rate, count):
    norm = jnp.sqrt(-jnp.expm1(-2.0 * decay_rate))
    weight = residues * norm
    steps = jnp.arange(count).astype(jnp.float32)
    return lax.optimization_barrier(jnp.sum(weight[:, :, None] * jnp.exp(-decay_rate[:, :, None] * steps), axis=0))

def toeplitz(taps):
    count = taps.shape[1]
    lag = jnp.arange(count)[:, None] - jnp.arange(count)[None, :]
    picked = jnp.take(taps, jnp.clip(lag, 0, count - 1), axis=1)
    return jnp.where(lag >= 0, picked, jnp.zeros_like(picked))

def short_conv(padded, weights, count):
    width = weights.shape[0]
    total = jnp.zeros((count, weights.shape[1]), jnp.float32)
    for shift_at in range(width):
        begin = width - 1 - shift_at
        total = total + weights[shift_at][None, :] * padded[begin:begin + count]
    return total

def reference(query_in, key_in, value_in, residues, decay_rate, short_filter, skip_gain):
    taps = filter_taps(residues, decay_rate, SPAN)
    toe = toeplitz(taps)
    norm = jnp.sqrt(-jnp.expm1(-2.0 * decay_rate))
    weight = residues * norm
    steps = jnp.arange(SPAN).astype(jnp.float32)
    lead = weight[:, :, None] * jnp.exp(-decay_rate[:, :, None] * (steps + 1.0))
    tail = jnp.exp(-decay_rate[:, :, None] * (SPAN - 1.0 - steps))
    power = jnp.exp(-decay_rate * SPAN)
    high = lax.Precision.HIGHEST
    front = jnp.zeros((SHORT - 1, D), jnp.float32)
    q_short = short_conv(jnp.concatenate([front, query_in.astype(jnp.float32)], 0), short_filter[0], TOTAL)
    k_short = short_conv(jnp.concatenate([front, key_in.astype(jnp.float32)], 0), short_filter[1], TOTAL)
    v_short = short_conv(jnp.concatenate([front, value_in.astype(jnp.float32)], 0), short_filter[2], TOTAL)
    gated = k_short * v_short
    blocks = gated.reshape(TOTAL // SPAN, SPAN, FILTERS, GS)

    def step_block(state, block):
        local = jnp.einsum('gts,sgj->tgj', toe, block, precision=high)
        term = jnp.einsum('ngt,ngj->tgj', lead, state, precision=high)
        fresh = jnp.einsum('ngs,sgj->ngj', tail, block, precision=high)
        return (state * power[:, :, None] + fresh, local + term)
    start = jnp.zeros((MODES, FILTERS, GS), jnp.float32)
    _, convs = lax.scan(step_block, start, blocks)
    long_conv = convs.reshape(TOTAL, D)
    return (q_short * (long_conv + skip_gain[0][None, :] * gated)).astype(jnp.bfloat16)
```

```python
import functools

import jax
import jax.numpy as jnp
from jax import lax
from jax.experimental import pallas as pl
from jax.experimental.pallas import tpu as pltpu
from jax.sharding import PartitionSpec as P

LANES = 128
SUB = 8
F32 = jnp.float32
BF16 = jnp.bfloat16


def split2(x):
    hi = x.astype(BF16)
    return hi, (x - hi.astype(F32)).astype(BF16)


def expand(table, tile, lanes, size):
    groups = table.shape[1]
    row = lax.broadcasted_iota(jnp.int32, (groups, lanes), 0)
    col = lax.broadcasted_iota(jnp.int32, (groups, lanes), 1)
    pick = (row == tile * (lanes // size) + col // size).astype(BF16)
    one, rest = split2(table)
    two, three = split2(table - one.astype(F32))
    out = jnp.dot(one, pick, preferred_element_type=F32)
    out = out + jnp.dot(two, pick, preferred_element_type=F32)
    return out + jnp.dot(three, pick, preferred_element_type=F32)


def norm_of(decay):
    x = 2.0 * decay
    series = x * (1.0 - x * (0.5 - x * (1.0 / 6 - x * (1.0 / 24 - x * (1.0 / 120 - x * (1.0 / 720))))))
    return jnp.sqrt(series)


def short3(x, before, taps):
    full = jnp.concatenate([before, x], 0)
    one = pltpu.roll(full, 1, 0)[SUB:]
    two = pltpu.roll(full, 2, 0)[SUB:]
    return taps[0] * x + taps[1] * one + taps[2] * two


def state_kernel(size, halo_ref, k_ref, v_ref, sf_ref, decay_ref, gated_ref, fresh_ref, spread_ref):
    length, lanes = k_ref.shape
    modes = decay_ref.shape[0]
    first = lax.axis_index("ctx") > 0
    keep = jnp.where(first, 1.0, 0.0).astype(F32)
    rates = expand(decay_ref[...], pl.program_id(0), lanes, size)
    spread_ref[...] = rates
    for part in range(lanes // LANES):
        at = slice(part * LANES, (part + 1) * LANES)
        rate = rates[:, at]
        step8 = jnp.exp(-float(SUB) * rate)
        step8 = [jnp.broadcast_to(step8[n : n + 1], (SUB, LANES)) for n in range(modes)]
        kt = [sf_ref[1, i : i + 1, at] for i in range(3)]
        vt = [sf_ref[2, i : i + 1, at] for i in range(3)]
        k_before = halo_ref[2 * SUB : 4 * SUB, at].astype(F32)[SUB:] * keep
        v_before = halo_ref[4 * SUB : 6 * SUB, at].astype(F32)[SUB:] * keep

        def step(i, carry):
            k_before, v_before, acc = carry
            rows = pl.ds(pl.multiple_of(i * 2 * SUB, 2 * SUB), 2 * SUB)
            k = k_ref[rows, at].astype(F32)
            v = v_ref[rows, at].astype(F32)
            gated = short3(k, k_before, kt) * short3(v, v_before, vt)
            gated_ref[rows, at] = gated
            for half in range(2):
                x = gated[half * SUB : (half + 1) * SUB]
                acc = [a * s + x for a, s in zip(acc, step8)]
            return k[SUB:], v[SUB:], acc

        zero = jnp.zeros((SUB, LANES), F32)
        _, _, acc = lax.fori_loop(
            0, length // (2 * SUB), step, (k_before, v_before, [zero] * modes), unroll=4
        )
        back = (SUB - 1 - lax.broadcasted_iota(jnp.int32, (SUB, LANES), 0)).astype(F32)
        for n in range(modes):
            weighted = acc[n] * jnp.exp(-rate[n : n + 1] * back)
            fresh_ref[n : n + 1, at] = jnp.sum(weighted, axis=0, keepdims=True)


def fold8(parts):
    sub = lax.broadcasted_iota(jnp.int32, parts[0].shape, 0)

    def join(a, b, gap):
        low = (sub // gap) % 2 == 0
        return jnp.where(low, a + pltpu.roll(a, SUB - gap, 0), b + pltpu.roll(b, gap, 0))

    parts = [join(parts[t], parts[t + 4], 4) for t in range(4)]
    parts = [join(parts[t], parts[t + 2], 2) for t in range(2)]
    return join(parts[0], parts[1], 1)


def local_kernel(size, first_tile, gated_ref, spread_ref, res_ref, skip_ref, out_ref):
    length, lanes = gated_ref.shape
    modes = res_ref.shape[0]
    rate = spread_ref[...]
    weight = expand(res_ref[...], first_tile + pl.program_id(0), lanes, size) * norm_of(rate)
    ratio = jnp.exp(-rate)
    skip = skip_ref[...]

    def step(i, state):
        base = pl.multiple_of(i * SUB, SUB)
        parts = []
        for t in range(SUB):
            x = gated_ref[pl.ds(base + t, 1), :]
            state = state * ratio + x
            mixed = state * weight
            total = mixed[:SUB]
            for at in range(SUB, modes, SUB):
                total = total + mixed[at : at + SUB]
            parts.append(total)
        rows = pl.ds(base, SUB)
        out_ref[rows, :] = fold8(parts) + skip * gated_ref[rows, :]
        return state

    lax.fori_loop(0, length // SUB, step, jnp.zeros((modes, lanes), F32))


def lead_kernel(size, res_ref, decay_ref, hi_ref, lo_ref):
    length, lanes = hi_ref.shape
    modes = decay_ref.shape[0]
    lane = lax.broadcasted_iota(jnp.int32, (modes, lanes), 1)
    own = lane % size == lax.broadcasted_iota(jnp.int32, (modes, lanes), 0)

    def row(table):
        wide = expand(table, pl.program_id(0), lanes, size)
        return jnp.sum(jnp.where(own, wide, 0.0), axis=0, keepdims=True)

    rate = row(decay_ref[...])
    weight = row(res_ref[...]) * norm_of(rate)
    steps = lax.broadcasted_iota(jnp.int32, (length, lanes), 0).astype(F32) + 1.0
    hi, lo = split2(weight * jnp.exp(-rate * steps))
    hi_ref[...] = hi
    lo_ref[...] = lo


def mix_kernel(size, bit, halo_ref, q_ref, sf_ref, spread_ref, prefix_ref, got_ref, local_ref, hi_ref, lo_ref, out_ref):
    length, lanes = q_ref.shape
    modes = spread_ref.shape[0]
    me = lax.axis_index("ctx")
    keep = jnp.where(me > 0, 1.0, 0.0).astype(F32)
    upper = jnp.where((me // bit) % 2 == 1, 1.0, 0.0).astype(F32)
    gap = (me % bit * length).astype(F32)
    state = prefix_ref[...] + jnp.exp(-spread_ref[...] * gap) * (got_ref[...] * upper)
    groups = lanes // size
    rows = groups * modes
    row = lax.broadcasted_iota(jnp.int32, (rows, lanes), 0)
    col = lax.broadcasted_iota(jnp.int32, (rows, lanes), 1)
    wide = jnp.where(row // modes == col // size, jnp.concatenate([state] * groups, 0), 0.0)
    hi, lo = split2(wide)
    term = jnp.dot(hi_ref[...], hi, preferred_element_type=F32)
    term = term + jnp.dot(lo_ref[...], hi, preferred_element_type=F32)
    term = term + jnp.dot(hi_ref[...], lo, preferred_element_type=F32)
    before = halo_ref[...].astype(F32)[SUB:] * keep
    q_short = short3(q_ref[...].astype(F32), before, [sf_ref[0, i : i + 1, :] for i in range(3)])
    out_ref[...] = (q_short * (local_ref[...] + term)).astype(BF16)


def body(query_in, key_in, value_in, residues, decay_rate, short_filter, skip_gain):
    length, width = query_in.shape
    modes, groups = residues.shape
    size = width // groups
    ranks = lax.axis_size("ctx")
    me = lax.axis_index("ctx")
    rim = 2 * SUB
    edge = length - rim
    rims = jnp.concatenate([query_in[edge:], key_in[edge:], value_in[edge:]], 0)
    with jax.named_scope("halo"):
        halo = lax.ppermute(rims, "ctx", [(i, (i + 1) % ranks) for i in range(ranks)])

    tile = min(width, 2 * LANES)
    grid = width // tile
    whole = lambda a: pl.BlockSpec(a.shape, lambda j: (0,) * a.ndim)
    cols = lambda rows, lanes, first=0: pl.BlockSpec((rows, lanes), lambda j: (0, j + first))
    taps_spec = lambda lanes: pl.BlockSpec((3, 3, lanes), lambda j: (0, 0, j))

    lead_shape = jax.ShapeDtypeStruct((length, groups * modes), BF16)
    lead_hi, lead_lo = pl.pallas_call(
        functools.partial(lead_kernel, size),
        grid=(groups * modes // tile,),
        in_specs=[whole(residues), whole(decay_rate)],
        out_specs=[cols(length, tile)] * 2,
        out_shape=[lead_shape] * 2,
        name="lead",
    )(residues, decay_rate)

    gated, fresh, spread = pl.pallas_call(
        functools.partial(state_kernel, size),
        grid=(grid,),
        in_specs=[cols(3 * rim, tile), cols(length, tile), cols(length, tile), taps_spec(tile), whole(decay_rate)],
        out_specs=[cols(length, tile), cols(modes, tile), cols(modes, tile)],
        out_shape=[
            jax.ShapeDtypeStruct((length, width), F32),
            jax.ShapeDtypeStruct((modes, width), F32),
            jax.ShapeDtypeStruct((modes, width), F32),
        ],
        name="state",
    )(halo, key_in, value_in, short_filter, decay_rate)

    local = pl.pallas_call(
        functools.partial(local_kernel, size, 0),
        grid=(grid,),
        in_specs=[cols(length, tile), cols(modes, tile), whole(residues), cols(1, tile)],
        out_specs=cols(length, tile),
        out_shape=jax.ShapeDtypeStruct((length, width), F32),
        name="local",
    )(gated, spread, residues, skip_gain)

    total, prefix, bit = fresh, jnp.zeros_like(fresh), 1
    while bit < ranks:
        with jax.named_scope("scan%d" % bit):
            got = lax.ppermute(total, "ctx", [(i, i ^ bit) for i in range(ranks)])
        if bit * 2 < ranks:
            upper = (me // bit) % 2 == 1
            span = jnp.exp(-spread * float(length * bit))
            reach = jnp.exp(-spread * (length * (me % bit)).astype(F32))
            prefix = prefix + jnp.where(upper, reach * got, 0.0)
            total = jnp.where(upper, total + span * got, got + span * total)
        bit *= 2

    return pl.pallas_call(
        functools.partial(mix_kernel, size, bit // 2),
        grid=(grid,),
        in_specs=[
            cols(rim, tile),
            cols(length, tile),
            taps_spec(tile),
            cols(modes, tile),
            cols(modes, tile),
            cols(modes, tile),
            cols(length, tile),
            cols(length, tile),
            cols(length, tile),
        ],
        out_specs=cols(length, tile),
        out_shape=jax.ShapeDtypeStruct((length, width), BF16),
        name="mix",
    )(halo, query_in, short_filter, spread, prefix, got, local, lead_hi, lead_lo)


def solution(mesh):
    placed = (
        P("ctx", "fsdp"),
        P("ctx", "fsdp"),
        P("ctx", "fsdp"),
        P(None, "fsdp"),
        P(None, "fsdp"),
        P(None, None, "fsdp"),
        P(None, "fsdp"),
    )
    return jax.shard_map(
        body, mesh=mesh, in_specs=placed, out_specs=P("ctx", "fsdp"), check_vma=False
    )
```

```python
import functools

import jax
import jax.numpy as jnp
from jax import lax
from jax.experimental import pallas as pl
from jax.experimental.pallas import tpu as pltpu
from jax.sharding import PartitionSpec as P


LANES = 128
WIDE = 256
SUB = 8
RIM = 16
F32 = jnp.float32
BF16 = jnp.bfloat16
VMEM = pl.BlockSpec(memory_space=pltpu.VMEM)
PARAMS = pltpu.CompilerParams(vmem_limit_bytes=8 << 20)


def split2(x):
    hi = x.astype(BF16)
    return hi, (x - hi.astype(F32)).astype(BF16)


def expand(table, first, lanes, size):
    groups = table.shape[1]
    row = lax.broadcasted_iota(jnp.int32, (groups, lanes), 0)
    col = lax.broadcasted_iota(jnp.int32, (groups, lanes), 1)
    pick = (row == first + col // size).astype(BF16)
    one, _ = split2(table)
    two, three = split2(table - one.astype(F32))
    out = jnp.dot(one, pick, preferred_element_type=F32)
    out = out + jnp.dot(two, pick, preferred_element_type=F32)
    return out + jnp.dot(three, pick, preferred_element_type=F32)


def norm_of(decay):
    x = 2.0 * decay
    total = jnp.full_like(x, 1.0)
    for k in range(9, 1, -1):
        total = 1.0 - x * total * (1.0 / k)
    return jnp.sqrt(x * total)


def short3(ref, start, count, taps):
    at = SUB + start
    out = taps[0] * ref[at : at + count]
    out = out + taps[1] * ref[at - 1 : at - 1 + count]
    return out + taps[2] * ref[at - 2 : at - 2 + count]


def rim_kernel(q_ref, k_ref, v_ref, out_ref, sem):
    copies = []
    for i, ref in enumerate((q_ref, k_ref, v_ref)):
        rim = ref.at[ref.shape[0] - RIM :]
        copies.append(pltpu.make_async_copy(rim, out_ref.at[i * RIM : (i + 1) * RIM], sem.at[i]))
        copies[i].start()
    for copy in copies:
        copy.wait()


def table_kernel(res_ref, decay_ref, lead_hi, lead_lo, tail_hi, tail_lo, spread_ref, span_ref, reach_ref):
    length, width = lead_hi.shape
    modes = decay_ref.shape[0]
    phases = span_ref.shape[0]
    me = lax.axis_index("ctx")
    lane = lax.broadcasted_iota(jnp.int32, (modes, LANES), 1)
    own = lane % modes == lax.broadcasted_iota(jnp.int32, (modes, LANES), 0)
    down = lax.broadcasted_iota(jnp.int32, (LANES, LANES), 0).astype(F32)
    along = lax.broadcasted_iota(jnp.int32, (LANES, LANES), 1).astype(F32)
    for tile in range(width // LANES):
        at = slice(tile * LANES, (tile + 1) * LANES)
        rates = expand(decay_ref[...], tile * (LANES // modes), LANES, modes)
        gains = expand(res_ref[...], tile * (LANES // modes), LANES, modes) * norm_of(rates)
        rate = jnp.sum(jnp.where(own, rates, 0.0), axis=0, keepdims=True)
        gain = jnp.sum(jnp.where(own, gains, 0.0), axis=0, keepdims=True)
        spread_ref[:, at] = rates
        for b in range(phases):
            upper = jnp.where((me >> b) % 2 == 1, 1.0, 0.0).astype(F32)
            gap = (me % (1 << b) * length).astype(F32)
            span_ref[b, :, at] = jnp.exp(-rates * float(length << b))
            reach_ref[b, :, at] = jnp.exp(-rates * gap) * upper
        lead = gain * jnp.exp(-rate * (down + 1.0))
        hop = jnp.exp(-rate * float(LANES))
        rate_rows = jnp.transpose(jnp.broadcast_to(rate, (LANES, LANES)))
        tail = jnp.exp(-rate_rows * (LANES - 1.0 - along))
        hop_rows = jnp.exp(-rate_rows * float(LANES))
        for c in range(length // LANES):
            rows = slice(c * LANES, (c + 1) * LANES)
            back = slice(length - (c + 1) * LANES, length - c * LANES)
            hi, lo = split2(lead)
            lead_hi[rows, at], lead_lo[rows, at] = hi, lo
            hi, lo = split2(tail)
            tail_hi[at, back], tail_lo[at, back] = hi, lo
            lead = lead * hop
            tail = tail * hop_rows


def state_kernel(size, halo_ref, k_ref, v_ref, sf_ref, tail_hi, tail_lo, gated_ref, fresh_ref, kf, vf, xh, xl):
    length, lanes = k_ref.shape
    modes = fresh_ref.shape[0]
    tile = pl.program_id(0)
    keep = jnp.where(lax.axis_index("ctx") > 0, 1.0, 0.0).astype(F32)
    row = lax.broadcasted_iota(jnp.int32, (modes, LANES), 1) // size
    for part in range(lanes // LANES):
        at = slice(part * LANES, (part + 1) * LANES)
        base = pl.multiple_of(tile * lanes + part * LANES, LANES)
        kf[0:SUB] = halo_ref[RIM : 2 * RIM, at].astype(F32)[SUB:] * keep
        vf[0:SUB] = halo_ref[2 * RIM : 3 * RIM, at].astype(F32)[SUB:] * keep
        kt = [sf_ref[1, i : i + 1, at] for i in range(3)]
        vt = [sf_ref[2, i : i + 1, at] for i in range(3)]
        piece = 64
        for start in range(0, length, piece):
            rows = slice(start, start + piece)
            kf[SUB + start : SUB + start + piece] = k_ref[rows, at].astype(F32)
            vf[SUB + start : SUB + start + piece] = v_ref[rows, at].astype(F32)
            gated = short3(kf, start, piece, kt) * short3(vf, start, piece, vt)
            gated_ref[rows, pl.ds(base, LANES)] = gated
            xh[rows], xl[rows] = split2(gated)
        table = pl.ds(base, LANES)
        out = jnp.dot(tail_hi[table, :], xh[...], preferred_element_type=F32)
        out = out + jnp.dot(tail_lo[table, :], xh[...], preferred_element_type=F32)
        out = out + jnp.dot(tail_hi[table, :], xl[...], preferred_element_type=F32)
        total = jnp.zeros((modes, LANES), F32)
        for g in range(LANES // size):
            total = jnp.where(row == g, out[g * modes : (g + 1) * modes], total)
        fresh_ref[:, pl.ds(base, LANES)] = total


def fold8(parts):
    sub = lax.broadcasted_iota(jnp.int32, parts[0].shape, 0)

    def join(a, b, gap):
        low = (sub // gap) % 2 == 0
        return jnp.where(low, a + pltpu.roll(a, SUB - gap, 0), b + pltpu.roll(b, gap, 0))

    parts = [join(parts[t], parts[t + 4], 4) for t in range(4)]
    parts = [join(parts[t], parts[t + 2], 2) for t in range(2)]
    return join(parts[0], parts[1], 1)


def local_kernel(size, first, gated_ref, spread_ref, res_ref, skip_ref, out_ref):
    length, lanes = out_ref.shape
    modes = res_ref.shape[0]
    at = slice(first, first + lanes)
    rate = spread_ref[:, at]
    weight = expand(res_ref[...], first // size, lanes, size) * norm_of(rate)
    ratio = jnp.exp(-rate)
    skip = skip_ref[:, at]

    def step(i, state):
        base = pl.multiple_of(i * SUB, SUB)
        parts = []
        for t in range(SUB):
            x = gated_ref[pl.ds(base + t, 1), at]
            state = state * ratio + x
            mixed = state * weight
            total = mixed[:SUB]
            for m in range(SUB, modes, SUB):
                total = total + mixed[m : m + SUB]
            parts.append(total)
        rows = pl.ds(base, SUB)
        out_ref[rows, :] = fold8(parts) + skip * gated_ref[rows, at]
        return state

    lax.fori_loop(0, length // SUB, step, jnp.zeros((modes, lanes), F32))


def mix_kernel(size, phases, parts, *refs):
    halo_ref, q_ref, sf_ref, reach_ref, lead_hi, lead_lo = refs[:6]
    gots = refs[6 : 6 + phases]
    locals_ = refs[6 + phases : 6 + phases + parts]
    out_ref, qf, stage, sem = refs[6 + phases + parts :]
    length, width = q_ref.shape
    modes = reach_ref.shape[1]
    keep = jnp.where(lax.axis_index("ctx") > 0, 1.0, 0.0).astype(F32)
    where = []
    for ref in locals_:
        where += [(ref, c) for c in range(0, ref.shape[1], LANES)]
    span = min(WIDE, width)
    groups = span // size
    row = lax.broadcasted_iota(jnp.int32, (groups * modes, span), 0)
    col = lax.broadcasted_iota(jnp.int32, (groups * modes, span), 1)
    block = row // modes == col // size
    copies = []
    for tile in range(width // span):
        at = slice(tile * span, (tile + 1) * span)
        state = reach_ref[0, :, at] * gots[0][:, at]
        for b in range(1, phases):
            state = state + reach_ref[b, :, at] * gots[b][:, at]
        wide = jnp.where(block, jnp.concatenate([state] * groups, 0), 0.0)
        hi, lo = split2(wide)
        term = jnp.dot(lead_hi[:, at], hi, preferred_element_type=F32)
        term = term + jnp.dot(lead_lo[:, at], hi, preferred_element_type=F32)
        term = term + jnp.dot(lead_hi[:, at], lo, preferred_element_type=F32)
        for half in range(span // LANES):
            lane = tile * span + half * LANES
            cut = slice(lane, lane + LANES)
            qf[0:SUB] = halo_ref[0:RIM, cut].astype(F32)[SUB:] * keep
            qf[SUB:] = q_ref[:, cut].astype(F32)
            taps = [sf_ref[0, i : i + 1, cut] for i in range(3)]
            near, c = where[lane // LANES]
            own = near[:, c : c + LANES] + term[:, half * LANES : (half + 1) * LANES]
            stage[:, cut] = (short3(qf, 0, length, taps) * own).astype(BF16)
        copy = pltpu.make_async_copy(stage.at[:, at], out_ref.at[:, at], sem.at[tile])
        copy.start()
        copies.append(copy)
    for copy in copies:
        copy.wait()


def body(query_in, key_in, value_in, residues, decay_rate, short_filter, skip_gain):
    length, width = query_in.shape
    modes, groups = residues.shape
    size = width // groups
    ranks = lax.axis_size("ctx")
    phases = ranks.bit_length() - 1
    rims = pl.pallas_call(
        rim_kernel,
        in_specs=[pl.BlockSpec(memory_space=pltpu.HBM)] * 3,
        out_specs=VMEM,
        out_shape=jax.ShapeDtypeStruct((3 * RIM, width), BF16),
        scratch_shapes=[pltpu.SemaphoreType.DMA((3,))],
        compiler_params=pltpu.CompilerParams(vmem_limit_bytes=60 << 20),
        name="rim",
    )(query_in, key_in, value_in)
    halo = lax.ppermute(rims, "ctx", [(i, (i + 1) % ranks) for i in range(ranks)])

    lead_shape = jax.ShapeDtypeStruct((length, width), BF16)
    tail_shape = jax.ShapeDtypeStruct((width, length), BF16)
    scan_shape = jax.ShapeDtypeStruct((phases, modes, width), F32)
    row_shape = jax.ShapeDtypeStruct((modes, width), F32)
    lead_hi, lead_lo, tail_hi, tail_lo, spread, span, reach = pl.pallas_call(
        table_kernel,
        in_specs=[VMEM] * 2,
        out_specs=[VMEM] * 7,
        out_shape=[lead_shape, lead_shape, tail_shape, tail_shape, row_shape, scan_shape, scan_shape],
        compiler_params=PARAMS,
        cost_estimate=pl.CostEstimate(flops=10**7, bytes_accessed=5 << 20, transcendentals=0),
        name="tables",
    )(residues, decay_rate)

    tile = min(width, WIDE)
    cols = lambda rows: pl.BlockSpec((rows, tile), lambda j: (0, j))
    gated, fresh = pl.pallas_call(
        functools.partial(state_kernel, size),
        grid=(width // tile,),
        in_specs=[
            cols(3 * RIM),
            cols(length),
            cols(length),
            pl.BlockSpec((3, 3, tile), lambda j: (0, 0, j)),
            VMEM,
            VMEM,
        ],
        out_specs=[VMEM] * 2,
        out_shape=[jax.ShapeDtypeStruct((length, width), F32), row_shape],
        scratch_shapes=[
            pltpu.VMEM((SUB + length, LANES), F32),
            pltpu.VMEM((SUB + length, LANES), F32),
            pltpu.VMEM((length, LANES), BF16),
            pltpu.VMEM((length, LANES), BF16),
        ],
        compiler_params=PARAMS,
        name="state",
    )(halo, key_in, value_in, short_filter, tail_hi, tail_lo)

    unit = LANES if width // LANES >= 2 * phases else min(width, WIDE)
    cuts = [width // unit * b // phases * unit for b in range(phases + 1)]
    nears, gots, total = [], [], fresh
    for b in range(phases):
        got = lax.ppermute(total, "ctx", [(i, i ^ (1 << b)) for i in range(ranks)])
        gots.append(got)
        lanes = cuts[b + 1] - cuts[b]
        if lanes:
            nears.append(
                pl.pallas_call(
                    functools.partial(local_kernel, size, cuts[b]),
                    in_specs=[VMEM] * 4,
                    out_specs=VMEM,
                    out_shape=jax.ShapeDtypeStruct((length, lanes), F32),
                    compiler_params=PARAMS,
                    cost_estimate=pl.CostEstimate(flops=10**7, bytes_accessed=4 << 20, transcendentals=0),
                    name="near",
                )(gated, spread, residues, skip_gain)
            )
        if b + 1 < phases:
            upper = (lax.axis_index("ctx") >> b) % 2 == 1
            total = jnp.where(upper, total + span[b] * got, got + span[b] * total)

    return pl.pallas_call(
        functools.partial(mix_kernel, size, phases, len(nears)),
        in_specs=[VMEM] * (6 + phases + len(nears)),
        out_specs=pl.BlockSpec(memory_space=pl.ANY),
        out_shape=jax.ShapeDtypeStruct((length, width), BF16),
        scratch_shapes=[
            pltpu.VMEM((SUB + length, LANES), F32),
            pltpu.VMEM((length, width), BF16),
            pltpu.SemaphoreType.DMA((max(1, width // WIDE),)),
        ],
        compiler_params=PARAMS,
        name="mix",
    )(halo, query_in, short_filter, reach, lead_hi, lead_lo, *gots, *nears)


def solution(mesh):
    placed = (
        P("ctx", "fsdp"),
        P("ctx", "fsdp"),
        P("ctx", "fsdp"),
        P(None, "fsdp"),
        P(None, "fsdp"),
        P(None, None, "fsdp"),
        P(None, "fsdp"),
    )
    return jax.shard_map(
        body, mesh=mesh, in_specs=placed, out_specs=P("ctx", "fsdp"), check_vma=False
    )
```

```python
import functools

import jax
import jax.numpy as jnp
from jax import lax
from jax.experimental import pallas as pl
from jax.experimental.pallas import tpu as pltpu
from jax.sharding import PartitionSpec as P


LANES = 128
WIDE = 256
SUB = 8
RIM = 16
F32 = jnp.float32
BF16 = jnp.bfloat16
VMEM = pl.BlockSpec(memory_space=pltpu.VMEM)
PARAMS = pltpu.CompilerParams(vmem_limit_bytes=8 << 20)


def split2(x):
    hi = x.astype(BF16)
    return hi, (x - hi.astype(F32)).astype(BF16)


def expand(table, first, lanes, size):
    groups = table.shape[1]
    row = lax.broadcasted_iota(jnp.int32, (groups, lanes), 0)
    col = lax.broadcasted_iota(jnp.int32, (groups, lanes), 1)
    pick = (row == first + col // size).astype(BF16)
    one, _ = split2(table)
    two, three = split2(table - one.astype(F32))
    out = jnp.dot(one, pick, preferred_element_type=F32)
    out = out + jnp.dot(two, pick, preferred_element_type=F32)
    return out + jnp.dot(three, pick, preferred_element_type=F32)


def norm_of(decay):
    x = 2.0 * decay
    total = jnp.full_like(x, 1.0)
    for k in range(9, 1, -1):
        total = 1.0 - x * total * (1.0 / k)
    return jnp.sqrt(x * total)


def short3(ref, start, count, taps):
    at = SUB + start
    out = taps[0] * ref[at : at + count]
    out = out + taps[1] * ref[at - 1 : at - 1 + count]
    return out + taps[2] * ref[at - 2 : at - 2 + count]


def rim_kernel(q_ref, k_ref, v_ref, out_ref, sem):
    copies = []
    for i, ref in enumerate((q_ref, k_ref, v_ref)):
        rim = ref.at[ref.shape[0] - RIM :]
        copies.append(pltpu.make_async_copy(rim, out_ref.at[i * RIM : (i + 1) * RIM], sem.at[i]))
        copies[i].start()
    for copy in copies:
        copy.wait()


def table_kernel(res_ref, decay_ref, skip_ref, lead_hi, lead_lo, tail_hi, tail_lo, ratio_ref, gain_ref, plain_ref, seam_ref, span_ref, reach_ref):
    length, width = lead_hi.shape
    modes = decay_ref.shape[0]
    phases = reach_ref.shape[0]
    plain_ref[...] = skip_ref[...]
    me = lax.axis_index("ctx")
    lane = lax.broadcasted_iota(jnp.int32, (modes, LANES), 1)
    own = lane % modes == lax.broadcasted_iota(jnp.int32, (modes, LANES), 0)
    down = lax.broadcasted_iota(jnp.int32, (LANES, LANES), 0).astype(F32)
    along = lax.broadcasted_iota(jnp.int32, (LANES, LANES), 1).astype(F32)
    for tile in range(width // LANES):
        at = slice(tile * LANES, (tile + 1) * LANES)
        rates = expand(decay_ref[...], tile * (LANES // modes), LANES, modes)
        gains = expand(res_ref[...], tile * (LANES // modes), LANES, modes) * norm_of(rates)
        rate = jnp.sum(jnp.where(own, rates, 0.0), axis=0, keepdims=True)
        gain = jnp.sum(jnp.where(own, gains, 0.0), axis=0, keepdims=True)
        ratio_ref[:, at] = jnp.exp(-rates)
        gain_ref[:, at] = gains
        for i in range(2):
            seam_ref[i, :, at] = jnp.exp(-rates * (length - 1.0 - i))
        for b in range(phases):
            upper = jnp.where((me >> b) % 2 == 1, 1.0, 0.0).astype(F32)
            gap = (me % (1 << b) * length).astype(F32)
            if b + 1 < phases:
                span_ref[b, :, at] = jnp.exp(-rates * float(length << b))
            reach_ref[b, :, at] = jnp.exp(-rates * gap) * upper
        lead = gain * jnp.exp(-rate * (down + 1.0))
        hop = jnp.exp(-rate * float(LANES))
        rate_rows = jnp.transpose(jnp.broadcast_to(rate, (LANES, LANES)))
        tail = jnp.exp(-rate_rows * (LANES - 1.0 - along))
        hop_rows = jnp.exp(-rate_rows * float(LANES))
        for c in range(length // LANES):
            rows = slice(c * LANES, (c + 1) * LANES)
            back = slice(length - (c + 1) * LANES, length - c * LANES)
            hi, lo = split2(lead)
            lead_hi[rows, at], lead_lo[rows, at] = hi, lo
            hi, lo = split2(tail)
            tail_hi[at, back], tail_lo[at, back] = hi, lo
            lead = lead * hop
            tail = tail * hop_rows


def state_kernel(size, k_ref, v_ref, sf_ref, tail_hi, tail_lo, gated_ref, fresh_ref, kf, vf, xh, xl):
    length, lanes = k_ref.shape
    modes = fresh_ref.shape[0]
    tile = pl.program_id(0)
    row = lax.broadcasted_iota(jnp.int32, (modes, LANES), 1) // size
    piece = 64
    inner = lax.broadcasted_iota(jnp.int32, (piece, LANES), 0) >= 2
    kf[0:SUB] = jnp.zeros((SUB, LANES), F32)
    vf[0:SUB] = jnp.zeros((SUB, LANES), F32)
    for part in range(lanes // LANES):
        at = slice(part * LANES, (part + 1) * LANES)
        base = pl.multiple_of(tile * lanes + part * LANES, LANES)
        kt = [sf_ref[1, i : i + 1, at] for i in range(3)]
        vt = [sf_ref[2, i : i + 1, at] for i in range(3)]
        for start in range(0, length, piece):
            rows = slice(start, start + piece)
            kf[SUB + start : SUB + start + piece] = k_ref[rows, at].astype(F32)
            vf[SUB + start : SUB + start + piece] = v_ref[rows, at].astype(F32)
            gated = short3(kf, start, piece, kt) * short3(vf, start, piece, vt)
            if start == 0:
                gated = jnp.where(inner, gated, 0.0)
            gated_ref[rows, pl.ds(base, LANES)] = gated
            xh[rows], xl[rows] = split2(gated)
        table = pl.ds(base, LANES)
        out = jnp.dot(tail_hi[table, :], xh[...], preferred_element_type=F32)
        out = out + jnp.dot(tail_lo[table, :], xh[...], preferred_element_type=F32)
        out = out + jnp.dot(tail_hi[table, :], xl[...], preferred_element_type=F32)
        total = jnp.zeros((modes, LANES), F32)
        for g in range(LANES // size):
            total = jnp.where(row == g, out[g * modes : (g + 1) * modes], total)
        fresh_ref[:, pl.ds(base, LANES)] = total


def seam_kernel(halo_ref, k_ref, v_ref, sf_ref, seam_ref, fresh_ref, gated_ref, out_ref, whole_ref, kf, vf):
    keep = jnp.where(lax.axis_index("ctx") > 0, 1.0, 0.0).astype(F32)
    kf[0:SUB] = halo_ref[RIM : 2 * RIM].astype(F32)[SUB:] * keep
    vf[0:SUB] = halo_ref[2 * RIM : 3 * RIM].astype(F32)[SUB:] * keep
    kf[SUB:] = k_ref[0:RIM].astype(F32)[:SUB]
    vf[SUB:] = v_ref[0:RIM].astype(F32)[:SUB]
    kt = [sf_ref[1, i : i + 1, :] for i in range(3)]
    vt = [sf_ref[2, i : i + 1, :] for i in range(3)]
    head = short3(kf, 0, SUB, kt) * short3(vf, 0, SUB, vt)
    whole_ref[0:SUB] = head
    out_ref[...] = fresh_ref[...] + seam_ref[0] * head[0:1] + seam_ref[1] * head[1:2]


def merge_kernel(b, total_ref, got_ref, span_ref, out_ref):
    upper = (lax.axis_index("ctx") >> b) % 2 == 1
    total, got = total_ref[...], got_ref[...]
    late = jnp.where(upper, total, got)
    early = jnp.where(upper, got, total)
    out_ref[...] = late + span_ref[b] * early


def fold8(parts):
    sub = lax.broadcasted_iota(jnp.int32, parts[0].shape, 0)

    def join(a, b, gap):
        low = (sub // gap) % 2 == 0
        return jnp.where(low, a + pltpu.roll(a, SUB - gap, 0), b + pltpu.roll(b, gap, 0))

    parts = [join(parts[t], parts[t + 4], 4) for t in range(4)]
    parts = [join(parts[t], parts[t + 2], 2) for t in range(2)]
    return join(parts[0], parts[1], 1)


def local_kernel(first, gated_ref, ratio_ref, gain_ref, plain_ref, out_ref):
    length, lanes = out_ref.shape
    modes = ratio_ref.shape[0]
    at = slice(first, first + lanes)
    ratio = ratio_ref[:, at]
    weight = gain_ref[:, at]
    skip = plain_ref[:, at]

    def step(i, state):
        base = pl.multiple_of(i * SUB, SUB)
        parts = []
        for t in range(SUB):
            x = gated_ref[pl.ds(base + t, 1), at]
            state = state * ratio + x
            mixed = state * weight
            total = mixed[:SUB]
            for m in range(SUB, modes, SUB):
                total = total + mixed[m : m + SUB]
            parts.append(total)
        rows = pl.ds(base, SUB)
        out_ref[rows, :] = fold8(parts) + skip * gated_ref[rows, at]
        return state

    lax.fori_loop(0, length // SUB, step, jnp.zeros((modes, lanes), F32))


def mix_kernel(size, phases, parts, *refs):
    halo_ref, q_ref, sf_ref, reach_ref, lead_hi, lead_lo = refs[:6]
    gots = refs[6 : 6 + phases]
    locals_ = refs[6 + phases : 6 + phases + parts]
    out_ref, qf, stage, sem = refs[6 + phases + parts :]
    length, width = q_ref.shape
    modes = reach_ref.shape[1]
    keep = jnp.where(lax.axis_index("ctx") > 0, 1.0, 0.0).astype(F32)
    where = []
    for ref in locals_:
        where += [(ref, c) for c in range(0, ref.shape[1], LANES)]
    span = min(WIDE, width)
    groups = span // size
    row = lax.broadcasted_iota(jnp.int32, (groups * modes, span), 0)
    col = lax.broadcasted_iota(jnp.int32, (groups * modes, span), 1)
    block = row // modes == col // size
    copies = []
    for tile in range(width // span):
        at = slice(tile * span, (tile + 1) * span)
        state = reach_ref[0, :, at] * gots[0][:, at]
        for b in range(1, phases):
            state = state + reach_ref[b, :, at] * gots[b][:, at]
        wide = jnp.where(block, jnp.concatenate([state] * groups, 0), 0.0)
        hi, lo = split2(wide)
        term = jnp.dot(lead_hi[:, at], hi, preferred_element_type=F32)
        term = term + jnp.dot(lead_lo[:, at], hi, preferred_element_type=F32)
        term = term + jnp.dot(lead_hi[:, at], lo, preferred_element_type=F32)
        for half in range(span // LANES):
            lane = tile * span + half * LANES
            cut = slice(lane, lane + LANES)
            qf[0:SUB] = halo_ref[0:RIM, cut].astype(F32)[SUB:] * keep
            qf[SUB:] = q_ref[:, cut].astype(F32)
            taps = [sf_ref[0, i : i + 1, cut] for i in range(3)]
            near, c = where[lane // LANES]
            own = near[:, c : c + LANES] + term[:, half * LANES : (half + 1) * LANES]
            stage[:, cut] = (short3(qf, 0, length, taps) * own).astype(BF16)
        copy = pltpu.make_async_copy(stage.at[:, at], out_ref.at[:, at], sem.at[tile])
        copy.start()
        copies.append(copy)
    for copy in copies:
        copy.wait()


def body(query_in, key_in, value_in, residues, decay_rate, short_filter, skip_gain):
    length, width = query_in.shape
    modes, groups = residues.shape
    size = width // groups
    ranks = lax.axis_size("ctx")
    phases = ranks.bit_length() - 1
    rims = pl.pallas_call(
        rim_kernel,
        in_specs=[pl.BlockSpec(memory_space=pltpu.HBM)] * 3,
        out_specs=VMEM,
        out_shape=jax.ShapeDtypeStruct((3 * RIM, width), BF16),
        scratch_shapes=[pltpu.SemaphoreType.DMA((3,))],
        compiler_params=pltpu.CompilerParams(vmem_limit_bytes=4 << 20),
        name="rim",
    )(*[pltpu.with_memory_space_constraint(a, pltpu.HBM) for a in (query_in, key_in, value_in)])
    halo = lax.ppermute(rims, "ctx", [(i, (i + 1) % ranks) for i in range(ranks)])

    lead_shape = jax.ShapeDtypeStruct((length, width), BF16)
    tail_shape = jax.ShapeDtypeStruct((width, length), BF16)
    scan_shape = lambda count: jax.ShapeDtypeStruct((count, modes, width), F32)
    row_shape = jax.ShapeDtypeStruct((modes, width), F32)
    lead_hi, lead_lo, tail_hi, tail_lo, ratio, gain, plain, seam, span, reach = pl.pallas_call(
        table_kernel,
        in_specs=[VMEM] * 3,
        out_specs=[VMEM] * 10,
        out_shape=[lead_shape] * 2
        + [tail_shape] * 2
        + [row_shape] * 2
        + [jax.ShapeDtypeStruct((1, width), F32), scan_shape(2), scan_shape(max(1, phases - 1)), scan_shape(phases)],
        compiler_params=PARAMS,
        cost_estimate=pl.CostEstimate(flops=10**7, bytes_accessed=5 << 20, transcendentals=0),
        name="tables",
    )(residues, decay_rate, skip_gain)

    tile = min(width, WIDE)
    cols = lambda rows: pl.BlockSpec((rows, tile), lambda j: (0, j))
    gated, fresh = pl.pallas_call(
        functools.partial(state_kernel, size),
        grid=(width // tile,),
        in_specs=[
            cols(length),
            cols(length),
            pl.BlockSpec((3, 3, tile), lambda j: (0, 0, j)),
            VMEM,
            VMEM,
        ],
        out_specs=[VMEM] * 2,
        out_shape=[jax.ShapeDtypeStruct((length, width), F32), row_shape],
        scratch_shapes=[
            pltpu.VMEM((SUB + length, LANES), F32),
            pltpu.VMEM((SUB + length, LANES), F32),
            pltpu.VMEM((length, LANES), BF16),
            pltpu.VMEM((length, LANES), BF16),
        ],
        compiler_params=PARAMS,
        cost_estimate=pl.CostEstimate(flops=10**7, bytes_accessed=5 << 20, transcendentals=0),
        name="state",
    )(key_in, value_in, short_filter, tail_hi, tail_lo)
    fresh, gated = pl.pallas_call(
        seam_kernel,
        in_specs=[VMEM] * 7,
        out_specs=[VMEM] * 2,
        out_shape=[row_shape, jax.ShapeDtypeStruct((length, width), F32)],
        input_output_aliases={6: 1},
        scratch_shapes=[pltpu.VMEM((2 * SUB, width), F32)] * 2,
        compiler_params=PARAMS,
        name="seam",
    )(halo, key_in, value_in, short_filter, seam, fresh, gated)

    unit = LANES if width // LANES >= 2 * phases else min(width, WIDE)
    cuts = [width // unit * b // phases * unit for b in range(phases + 1)]
    nears, gots, total = [], [], fresh
    for b in range(phases):
        got = lax.ppermute(total, "ctx", [(i, i ^ (1 << b)) for i in range(ranks)])
        gots.append(got)
        lanes = cuts[b + 1] - cuts[b]
        if lanes:
            nears.append(
                pl.pallas_call(
                    functools.partial(local_kernel, cuts[b]),
                    in_specs=[VMEM] * 4,
                    out_specs=VMEM,
                    out_shape=jax.ShapeDtypeStruct((length, lanes), F32),
                    compiler_params=PARAMS,
                    cost_estimate=pl.CostEstimate(flops=10**7, bytes_accessed=4 << 20, transcendentals=0),
                    name="near",
                )(gated, ratio, gain, plain)
            )
        if b + 1 < phases:
            total = pl.pallas_call(
                functools.partial(merge_kernel, b),
                in_specs=[VMEM] * 3,
                out_specs=VMEM,
                out_shape=row_shape,
                compiler_params=PARAMS,
                name="merge",
            )(total, got, span)

    return pl.pallas_call(
        functools.partial(mix_kernel, size, phases, len(nears)),
        in_specs=[VMEM] * (6 + phases + len(nears)),
        out_specs=pl.BlockSpec(memory_space=pl.ANY),
        out_shape=jax.ShapeDtypeStruct((length, width), BF16),
        scratch_shapes=[
            pltpu.VMEM((SUB + length, LANES), F32),
            pltpu.VMEM((length, width), BF16),
            pltpu.SemaphoreType.DMA((max(1, width // WIDE),)),
        ],
        compiler_params=PARAMS,
        name="mix",
    )(halo, query_in, short_filter, reach, lead_hi, lead_lo, *gots, *nears)


def solution(mesh):
    placed = (
        P("ctx", "fsdp"),
        P("ctx", "fsdp"),
        P("ctx", "fsdp"),
        P(None, "fsdp"),
        P(None, "fsdp"),
        P(None, None, "fsdp"),
        P(None, "fsdp"),
    )
    return jax.shard_map(
        body, mesh=mesh, in_specs=placed, out_specs=P("ctx", "fsdp"), check_vma=False
    )
```

```python
import functools

import jax
import jax.numpy as jnp
from jax import lax
from jax.experimental import pallas as pl
from jax.experimental.pallas import tpu as pltpu
from jax.sharding import PartitionSpec as P


LANES = 128
WIDE = 256
SUB = 8
RIM = 16
F32 = jnp.float32
BF16 = jnp.bfloat16
VMEM = pl.BlockSpec(memory_space=pltpu.VMEM)
PARAMS = pltpu.CompilerParams(vmem_limit_bytes=8 << 20)


def split2(x):
    hi = x.astype(BF16)
    return hi, (x - hi.astype(F32)).astype(BF16)


def expand(table, first, lanes, size):
    groups = table.shape[1]
    row = lax.broadcasted_iota(jnp.int32, (groups, lanes), 0)
    col = lax.broadcasted_iota(jnp.int32, (groups, lanes), 1)
    pick = (row == first + col // size).astype(BF16)
    one, _ = split2(table)
    two, three = split2(table - one.astype(F32))
    out = jnp.dot(one, pick, preferred_element_type=F32)
    out = out + jnp.dot(two, pick, preferred_element_type=F32)
    return out + jnp.dot(three, pick, preferred_element_type=F32)


def norm_of(decay):
    x = 2.0 * decay
    total = jnp.full_like(x, 1.0)
    for k in range(9, 1, -1):
        total = 1.0 - x * total * (1.0 / k)
    return jnp.sqrt(x * total)


def short3(ref, start, count, taps):
    at = SUB + start
    out = taps[0] * ref[at : at + count]
    out = out + taps[1] * ref[at - 1 : at - 1 + count]
    return out + taps[2] * ref[at - 2 : at - 2 + count]


def rim_kernel(q_ref, k_ref, v_ref, out_ref, sem):
    copies = []
    for i, ref in enumerate((q_ref, k_ref, v_ref)):
        rim = ref.at[ref.shape[0] - RIM :]
        copies.append(pltpu.make_async_copy(rim, out_ref.at[i * RIM : (i + 1) * RIM], sem.at[i]))
        copies[i].start()
    for copy in copies:
        copy.wait()


def table_kernel(res_ref, decay_ref, skip_ref, lead_hi, lead_lo, tail_ref, row_ref, plain_ref, hop_ref, seam_ref, span_ref, reach_ref):
    length, width = lead_hi.shape
    modes = decay_ref.shape[0]
    phases = reach_ref.shape[0]
    plain_ref[...] = skip_ref[...]
    me = lax.axis_index("ctx")
    lane = lax.broadcasted_iota(jnp.int32, (modes, LANES), 1)
    own = lane % modes == lax.broadcasted_iota(jnp.int32, (modes, LANES), 0)
    down = lax.broadcasted_iota(jnp.int32, (LANES, LANES), 0).astype(F32)
    along = lax.broadcasted_iota(jnp.int32, (LANES, LANES), 1).astype(F32)
    for tile in range(width // LANES):
        at = slice(tile * LANES, (tile + 1) * LANES)
        rates = expand(decay_ref[...], tile * (LANES // modes), LANES, modes)
        gains = expand(res_ref[...], tile * (LANES // modes), LANES, modes) * norm_of(rates)
        rate = jnp.sum(jnp.where(own, rates, 0.0), axis=0, keepdims=True)
        gain = jnp.sum(jnp.where(own, gains, 0.0), axis=0, keepdims=True)
        row_ref[0:1, at] = rate
        row_ref[1:2, at] = gain
        hop_ref[:, at] = jnp.exp(-rates * float(LANES))
        for i in range(2):
            seam_ref[i, :, at] = jnp.exp(-rates * (LANES - 1.0 - i))
        for b in range(phases):
            upper = jnp.where((me >> b) % 2 == 1, 1.0, 0.0).astype(F32)
            gap = (me % (1 << b) * length).astype(F32)
            if b + 1 < phases:
                span_ref[b, :, at] = jnp.exp(-rates * float(length << b))
            reach_ref[b, :, at] = jnp.exp(-rates * gap) * upper
        rate_rows = jnp.transpose(jnp.broadcast_to(rate, (LANES, LANES)))
        tail_ref[at, 0:LANES], tail_ref[at, LANES:] = split2(jnp.exp(-rate_rows * (LANES - 1.0 - along)))
        lead = gain * jnp.exp(-rate * (down + 1.0))
        hop = jnp.exp(-rate * float(LANES))
        for c in range(length // LANES):
            rows = slice(c * LANES, (c + 1) * LANES)
            lead_hi[rows, at], lead_lo[rows, at] = split2(lead)
            lead = lead * hop


def state_kernel(size, k_ref, v_ref, sf_ref, tail_ref, hop_ref, gated_ref, fresh_ref, enter_ref, kf, vf):
    length, lanes = k_ref.shape
    modes = fresh_ref.shape[0]
    tile = pl.program_id(0)
    row = lax.broadcasted_iota(jnp.int32, (modes, LANES), 1) // size
    piece = 64
    inner = lax.broadcasted_iota(jnp.int32, (piece, LANES), 0) >= 2
    kf[0:SUB] = jnp.zeros((SUB, LANES), F32)
    vf[0:SUB] = jnp.zeros((SUB, LANES), F32)
    for part in range(lanes // LANES):
        at = slice(part * LANES, (part + 1) * LANES)
        base = pl.multiple_of(tile * lanes + part * LANES, LANES)
        own = pl.ds(base, LANES)
        kt = [sf_ref[1, i : i + 1, at] for i in range(3)]
        vt = [sf_ref[2, i : i + 1, at] for i in range(3)]
        hop = hop_ref[:, own]
        tail, tail_hi = tail_ref[own, :], tail_ref[own, 0:LANES]
        total = jnp.zeros((modes, LANES), F32)
        for c in range(length // LANES):
            his, los = [], []
            for start in range(c * LANES, (c + 1) * LANES, piece):
                rows = slice(start, start + piece)
                kf[SUB + start : SUB + start + piece] = k_ref[rows, at].astype(F32)
                vf[SUB + start : SUB + start + piece] = v_ref[rows, at].astype(F32)
                gated = short3(kf, start, piece, kt) * short3(vf, start, piece, vt)
                if start == 0:
                    gated = jnp.where(inner, gated, 0.0)
                gated_ref[rows, own] = gated
                hi, lo = split2(gated)
                his.append(hi)
                los.append(lo)
            out = jnp.dot(tail, jnp.concatenate(his + his, 0), preferred_element_type=F32)
            out = out + jnp.dot(tail_hi, jnp.concatenate(los, 0), preferred_element_type=F32)
            fresh = jnp.zeros((modes, LANES), F32)
            for g in range(LANES // size):
                fresh = jnp.where(row == g, out[g * modes : (g + 1) * modes], fresh)
            if c:
                enter_ref[c - 1, :, own] = total
            total = total * hop + fresh
        fresh_ref[:, own] = total


def seam_kernel(halo_ref, k_ref, v_ref, sf_ref, seam_ref, hop_ref, fresh_ref, enter_ref, gated_ref, out_ref, into_ref, whole_ref, kf, vf):
    keep = jnp.where(lax.axis_index("ctx") > 0, 1.0, 0.0).astype(F32)
    kf[0:SUB] = halo_ref[RIM : 2 * RIM].astype(F32)[SUB:] * keep
    vf[0:SUB] = halo_ref[2 * RIM : 3 * RIM].astype(F32)[SUB:] * keep
    kf[SUB:] = k_ref[0:RIM].astype(F32)[:SUB]
    vf[SUB:] = v_ref[0:RIM].astype(F32)[:SUB]
    kt = [sf_ref[1, i : i + 1, :] for i in range(3)]
    vt = [sf_ref[2, i : i + 1, :] for i in range(3)]
    head = short3(kf, 0, SUB, kt) * short3(vf, 0, SUB, vt)
    whole_ref[0:SUB] = head
    first = seam_ref[0] * head[0:1] + seam_ref[1] * head[1:2]
    for c in range(enter_ref.shape[0]):
        into_ref[c] = enter_ref[c] + first
        first = first * hop_ref[...]
    out_ref[...] = fresh_ref[...] + first


def merge_kernel(b, total_ref, got_ref, span_ref, out_ref):
    upper = (lax.axis_index("ctx") >> b) % 2 == 1
    total, got = total_ref[...], got_ref[...]
    late = jnp.where(upper, total, got)
    early = jnp.where(upper, got, total)
    out_ref[...] = late + span_ref[b] * early


def near_kernel(size, first, gated_ref, into_ref, row_ref, plain_ref, lead_hi, lead_lo, out_ref):
    length, lanes = out_ref.shape
    modes = into_ref.shape[1]
    chunks = length // LANES
    groups = LANES // size
    down = lax.broadcasted_iota(jnp.int32, (LANES, LANES), 0)
    along = lax.broadcasted_iota(jnp.int32, (LANES, LANES), 1)
    causal = along >= down
    block = down // modes == along // size

    for tile in range(lanes // LANES):
        at = slice(first + tile * LANES, first + (tile + 1) * LANES)
        to = slice(tile * LANES, (tile + 1) * LANES)
        rate = jnp.transpose(jnp.broadcast_to(row_ref[0:1, at], (LANES, LANES)))
        gain = jnp.transpose(jnp.broadcast_to(row_ref[1:2, at], (LANES, LANES)))
        curve = gain * jnp.exp(-rate * along.astype(F32))
        halves = [split2(jnp.transpose(gated_ref[c * LANES : (c + 1) * LANES, at])) for c in range(chunks)]
        outs = []
        for g in range(groups):
            rows = slice(g * size, (g + 1) * size)
            taps = jnp.sum(curve[g * modes : (g + 1) * modes], axis=0, keepdims=True)
            toe = pltpu.roll(jnp.broadcast_to(taps, (LANES, LANES)), 0, 1, stride=1, stride_axis=0)
            hi, lo = split2(jnp.where(causal, toe, 0.0))
            xh = jnp.concatenate([h[rows] for h, _ in halves], 0)
            xl = jnp.concatenate([l[rows] for _, l in halves], 0)
            out = jnp.dot(jnp.concatenate([xh, xl], 1), jnp.concatenate([hi, hi], 0), preferred_element_type=F32)
            outs.append(out + jnp.dot(xh, lo, preferred_element_type=F32))
        lead = jnp.concatenate([lead_hi[0:LANES, at], lead_lo[0:LANES, at]], 1)
        for c in range(chunks):
            rows = slice(c * LANES, (c + 1) * LANES)
            near = jnp.transpose(jnp.concatenate([o[c * size : (c + 1) * size] for o in outs], 0))
            near = near + plain_ref[:, at] * gated_ref[rows, at]
            if c:
                wide = jnp.where(block, jnp.concatenate([into_ref[c - 1, :, at]] * groups, 0), 0.0)
                hi, lo = split2(wide)
                near = near + jnp.dot(lead, jnp.concatenate([hi, hi], 0), preferred_element_type=F32)
                near = near + jnp.dot(lead[:, :LANES], lo, preferred_element_type=F32)
            out_ref[rows, to] = near


def mix_kernel(size, phases, parts, *refs):
    halo_ref, q_ref, sf_ref, reach_ref, lead_hi, lead_lo = refs[:6]
    gots = refs[6 : 6 + phases]
    locals_ = refs[6 + phases : 6 + phases + parts]
    out_ref, qf, stage, sem = refs[6 + phases + parts :]
    length, width = q_ref.shape
    modes = reach_ref.shape[1]
    keep = jnp.where(lax.axis_index("ctx") > 0, 1.0, 0.0).astype(F32)
    where = []
    for ref in locals_:
        where += [(ref, c) for c in range(0, ref.shape[1], LANES)]
    span = min(WIDE, width)
    groups = span // size
    row = lax.broadcasted_iota(jnp.int32, (groups * modes, span), 0)
    col = lax.broadcasted_iota(jnp.int32, (groups * modes, span), 1)
    block = row // modes == col // size
    copies = []
    for tile in range(width // span):
        at = slice(tile * span, (tile + 1) * span)
        state = reach_ref[0, :, at] * gots[0][:, at]
        for b in range(1, phases):
            state = state + reach_ref[b, :, at] * gots[b][:, at]
        wide = jnp.where(block, jnp.concatenate([state] * groups, 0), 0.0)
        hi, lo = split2(wide)
        term = jnp.dot(lead_hi[:, at], hi, preferred_element_type=F32)
        term = term + jnp.dot(lead_lo[:, at], hi, preferred_element_type=F32)
        term = term + jnp.dot(lead_hi[:, at], lo, preferred_element_type=F32)
        for half in range(span // LANES):
            lane = tile * span + half * LANES
            cut = slice(lane, lane + LANES)
            qf[0:SUB] = halo_ref[0:RIM, cut].astype(F32)[SUB:] * keep
            qf[SUB:] = q_ref[:, cut].astype(F32)
            taps = [sf_ref[0, i : i + 1, cut] for i in range(3)]
            near, c = where[lane // LANES]
            own = near[:, c : c + LANES] + term[:, half * LANES : (half + 1) * LANES]
            stage[:, cut] = (short3(qf, 0, length, taps) * own).astype(BF16)
        copy = pltpu.make_async_copy(stage.at[:, at], out_ref.at[:, at], sem.at[tile])
        copy.start()
        copies.append(copy)
    for copy in copies:
        copy.wait()


def body(query_in, key_in, value_in, residues, decay_rate, short_filter, skip_gain):
    length, width = query_in.shape
    modes, groups = residues.shape
    size = width // groups
    ranks = lax.axis_size("ctx")
    phases = ranks.bit_length() - 1
    rims = pl.pallas_call(
        rim_kernel,
        in_specs=[pl.BlockSpec(memory_space=pltpu.HBM)] * 3,
        out_specs=VMEM,
        out_shape=jax.ShapeDtypeStruct((3 * RIM, width), BF16),
        scratch_shapes=[pltpu.SemaphoreType.DMA((3,))],
        compiler_params=pltpu.CompilerParams(vmem_limit_bytes=4 << 20),
        name="rim",
    )(*[pltpu.with_memory_space_constraint(a, pltpu.HBM) for a in (query_in, key_in, value_in)])
    halo = lax.ppermute(rims, "ctx", [(i, (i + 1) % ranks) for i in range(ranks)])

    lead_shape = jax.ShapeDtypeStruct((length, width), BF16)
    tail_shape = jax.ShapeDtypeStruct((width, 2 * LANES), BF16)
    scan_shape = lambda count: jax.ShapeDtypeStruct((count, modes, width), F32)
    row_shape = jax.ShapeDtypeStruct((modes, width), F32)
    lead_hi, lead_lo, tail, row, plain, hop, seam, span, reach = pl.pallas_call(
        table_kernel,
        in_specs=[VMEM] * 3,
        out_specs=[VMEM] * 9,
        out_shape=[
            lead_shape,
            lead_shape,
            tail_shape,
            jax.ShapeDtypeStruct((2, width), F32),
            jax.ShapeDtypeStruct((1, width), F32),
            row_shape,
            scan_shape(2),
            scan_shape(max(1, phases - 1)),
            scan_shape(phases),
        ],
        compiler_params=PARAMS,
        cost_estimate=pl.CostEstimate(flops=10**7, bytes_accessed=5 << 20, transcendentals=0),
        name="tables",
    )(residues, decay_rate, skip_gain)

    tile = min(width, WIDE)
    cols = lambda rows: pl.BlockSpec((rows, tile), lambda j: (0, j))
    gated_shape = jax.ShapeDtypeStruct((length, width), F32)
    enter_shape = scan_shape(length // LANES - 1)
    gated, fresh, enter = pl.pallas_call(
        functools.partial(state_kernel, size),
        grid=(width // tile,),
        in_specs=[
            cols(length),
            cols(length),
            pl.BlockSpec((3, 3, tile), lambda j: (0, 0, j)),
            VMEM,
            VMEM,
        ],
        out_specs=[VMEM] * 3,
        out_shape=[gated_shape, row_shape, enter_shape],
        scratch_shapes=[pltpu.VMEM((SUB + length, LANES), F32)] * 2,
        compiler_params=PARAMS,
        cost_estimate=pl.CostEstimate(flops=10**7, bytes_accessed=5 << 20, transcendentals=0),
        name="state",
    )(key_in, value_in, short_filter, tail, hop)
    fresh, into, gated = pl.pallas_call(
        seam_kernel,
        in_specs=[VMEM] * 9,
        out_specs=[VMEM] * 3,
        out_shape=[row_shape, enter_shape, gated_shape],
        input_output_aliases={8: 2},
        scratch_shapes=[pltpu.VMEM((2 * SUB, width), F32)] * 2,
        compiler_params=PARAMS,
        name="seam",
    )(halo, key_in, value_in, short_filter, seam, hop, fresh, enter, gated)

    unit = LANES if width // LANES >= 2 * phases else min(width, WIDE)
    cuts = [width // unit * b // phases * unit for b in range(phases + 1)]
    nears, gots, total = [], [], fresh
    for b in range(phases):
        got = lax.ppermute(total, "ctx", [(i, i ^ (1 << b)) for i in range(ranks)])
        gots.append(got)
        lanes = cuts[b + 1] - cuts[b]
        if lanes:
            nears.append(
                pl.pallas_call(
                    functools.partial(near_kernel, size, cuts[b]),
                    in_specs=[VMEM] * 6,
                    out_specs=VMEM,
                    out_shape=jax.ShapeDtypeStruct((length, lanes), F32),
                    compiler_params=PARAMS,
                    cost_estimate=pl.CostEstimate(flops=10**7, bytes_accessed=4 << 20, transcendentals=0),
                    name="near",
                )(gated, into, row, plain, lead_hi, lead_lo)
            )
        if b + 1 < phases:
            total = pl.pallas_call(
                functools.partial(merge_kernel, b),
                in_specs=[VMEM] * 3,
                out_specs=VMEM,
                out_shape=row_shape,
                compiler_params=PARAMS,
                name="merge",
            )(total, got, span)

    return pl.pallas_call(
        functools.partial(mix_kernel, size, phases, len(nears)),
        in_specs=[VMEM] * (6 + phases + len(nears)),
        out_specs=pl.BlockSpec(memory_space=pl.ANY),
        out_shape=jax.ShapeDtypeStruct((length, width), BF16),
        scratch_shapes=[
            pltpu.VMEM((SUB + length, LANES), F32),
            pltpu.VMEM((length, width), BF16),
            pltpu.SemaphoreType.DMA((max(1, width // WIDE),)),
        ],
        compiler_params=PARAMS,
        name="mix",
    )(halo, query_in, short_filter, reach, lead_hi, lead_lo, *gots, *nears)


def solution(mesh):
    placed = (
        P("ctx", "fsdp"),
        P("ctx", "fsdp"),
        P("ctx", "fsdp"),
        P(None, "fsdp"),
        P(None, "fsdp"),
        P(None, None, "fsdp"),
        P(None, "fsdp"),
    )
    return jax.shard_map(body, mesh=mesh, in_specs=placed, out_specs=P("ctx", "fsdp"), check_vma=False)
```

```python
import functools

import jax
import jax.numpy as jnp
from jax import lax
from jax.experimental import pallas as pl
from jax.experimental.pallas import tpu as pltpu
from jax.sharding import PartitionSpec as P


LANES = 128
WIDE = 256
SUB = 8
RIM = 8
F32 = jnp.float32
BF16 = jnp.bfloat16
VMEM = pl.BlockSpec(memory_space=pltpu.VMEM)
PARAMS = pltpu.CompilerParams(vmem_limit_bytes=8 << 20)


def split2(x):
    hi = x.astype(BF16)
    return hi, (x - hi.astype(F32)).astype(BF16)


def expand(table, first, lanes, size):
    groups = table.shape[1]
    row = lax.broadcasted_iota(jnp.int32, (groups, lanes), 0)
    col = lax.broadcasted_iota(jnp.int32, (groups, lanes), 1)
    pick = (row == first + col // size).astype(BF16)
    one, _ = split2(table)
    two, three = split2(table - one.astype(F32))
    out = jnp.dot(one, pick, preferred_element_type=F32)
    out = out + jnp.dot(two, pick, preferred_element_type=F32)
    return out + jnp.dot(three, pick, preferred_element_type=F32)


def norm_of(decay):
    x = 2.0 * decay
    total = jnp.full_like(x, 1.0)
    for k in range(9, 1, -1):
        total = 1.0 - x * total * (1.0 / k)
    return jnp.sqrt(x * total)


def short3(ref, start, count, taps):
    at = SUB + start
    out = taps[0] * ref[at : at + count]
    out = out + taps[1] * ref[at - 1 : at - 1 + count]
    return out + taps[2] * ref[at - 2 : at - 2 + count]


def rim_kernel(q_ref, k_ref, v_ref, out_ref, sem):
    copies = []
    for i, ref in enumerate((q_ref, k_ref, v_ref)):
        rim = ref.at[ref.shape[0] - RIM :]
        copies.append(pltpu.make_async_copy(rim, out_ref.at[i * RIM : (i + 1) * RIM], sem.at[i]))
        copies[i].start()
    for copy in copies:
        copy.wait()


def table_kernel(res_ref, decay_ref, skip_ref, lead_hi, lead_lo, tail_ref, row_ref, plain_ref, hop_ref, seam_ref, span_ref, reach_ref):
    length, width = lead_hi.shape
    modes = decay_ref.shape[0]
    phases = reach_ref.shape[0]
    plain_ref[...] = skip_ref[...]
    me = lax.axis_index("ctx")
    lane = lax.broadcasted_iota(jnp.int32, (modes, LANES), 1)
    own = lane % modes == lax.broadcasted_iota(jnp.int32, (modes, LANES), 0)
    down = lax.broadcasted_iota(jnp.int32, (LANES, LANES), 0).astype(F32)
    along = lax.broadcasted_iota(jnp.int32, (LANES, LANES), 1).astype(F32)
    for tile in range(width // LANES):
        at = slice(tile * LANES, (tile + 1) * LANES)
        rates = expand(decay_ref[...], tile * (LANES // modes), LANES, modes)
        gains = expand(res_ref[...], tile * (LANES // modes), LANES, modes) * norm_of(rates)
        rate = jnp.sum(jnp.where(own, rates, 0.0), axis=0, keepdims=True)
        gain = jnp.sum(jnp.where(own, gains, 0.0), axis=0, keepdims=True)
        row_ref[0:1, at] = rate
        row_ref[1:2, at] = gain
        hop_ref[:, at] = jnp.exp(-rates * float(LANES))
        for i in range(2):
            seam_ref[i, :, at] = jnp.exp(-rates * (LANES - 1.0 - i))
        for b in range(phases):
            upper = jnp.where((me >> b) % 2 == 1, 1.0, 0.0).astype(F32)
            gap = (me % (1 << b) * length).astype(F32)
            if b + 1 < phases:
                span_ref[b, :, at] = jnp.exp(-rates * float(length << b))
            reach_ref[b, :, at] = jnp.exp(-rates * gap) * upper
        rate_rows = jnp.transpose(jnp.broadcast_to(rate, (LANES, LANES)))
        tail_ref[at, 0:LANES], tail_ref[at, LANES:] = split2(jnp.exp(-rate_rows * (LANES - 1.0 - along)))
        lead = gain * jnp.exp(-rate * (down + 1.0))
        hop = jnp.exp(-rate * float(LANES))
        for c in range(length // LANES):
            rows = slice(c * LANES, (c + 1) * LANES)
            lead_hi[rows, at], lead_lo[rows, at] = split2(lead)
            lead = lead * hop


def state_kernel(size, k_ref, v_ref, sf_ref, tail_ref, hop_ref, gated_ref, fresh_ref, enter_ref, kf, vf):
    length, lanes = k_ref.shape
    modes = fresh_ref.shape[0]
    tile = pl.program_id(0)
    row = lax.broadcasted_iota(jnp.int32, (modes, LANES), 1) // size
    piece = 64
    inner = lax.broadcasted_iota(jnp.int32, (piece, LANES), 0) >= 2
    kf[0:SUB] = jnp.zeros((SUB, LANES), F32)
    vf[0:SUB] = jnp.zeros((SUB, LANES), F32)
    for part in range(lanes // LANES):
        at = slice(part * LANES, (part + 1) * LANES)
        base = pl.multiple_of(tile * lanes + part * LANES, LANES)
        own = pl.ds(base, LANES)
        kt = [sf_ref[1, i : i + 1, at] for i in range(3)]
        vt = [sf_ref[2, i : i + 1, at] for i in range(3)]
        hop = hop_ref[:, own]
        tail, tail_hi = tail_ref[own, :], tail_ref[own, 0:LANES]
        total = jnp.zeros((modes, LANES), F32)
        for c in range(length // LANES):
            his, los = [], []
            for start in range(c * LANES, (c + 1) * LANES, piece):
                rows = slice(start, start + piece)
                kf[SUB + start : SUB + start + piece] = k_ref[rows, at].astype(F32)
                vf[SUB + start : SUB + start + piece] = v_ref[rows, at].astype(F32)
                gated = short3(kf, start, piece, kt) * short3(vf, start, piece, vt)
                if start == 0:
                    gated = jnp.where(inner, gated, 0.0)
                gated_ref[rows, own] = gated
                hi, lo = split2(gated)
                his.append(hi)
                los.append(lo)
            out = jnp.dot(tail, jnp.concatenate(his + his, 0), preferred_element_type=F32)
            out = out + jnp.dot(tail_hi, jnp.concatenate(los, 0), preferred_element_type=F32)
            fresh = jnp.zeros((modes, LANES), F32)
            for g in range(LANES // size):
                fresh = jnp.where(row == g, out[g * modes : (g + 1) * modes], fresh)
            if c:
                enter_ref[c - 1, :, own] = total
            total = total * hop + fresh
        fresh_ref[:, own] = total


def seam_kernel(halo_ref, k_ref, v_ref, sf_ref, seam_ref, hop_ref, fresh_ref, enter_ref, gated_ref, out_ref, into_ref, whole_ref, kf, vf):
    keep = jnp.where(lax.axis_index("ctx") > 0, 1.0, 0.0).astype(F32)
    kf[0:SUB] = halo_ref[RIM : 2 * RIM].astype(F32) * keep
    vf[0:SUB] = halo_ref[2 * RIM : 3 * RIM].astype(F32) * keep
    kf[SUB:] = k_ref[0:SUB].astype(F32)
    vf[SUB:] = v_ref[0:SUB].astype(F32)
    kt = [sf_ref[1, i : i + 1, :] for i in range(3)]
    vt = [sf_ref[2, i : i + 1, :] for i in range(3)]
    head = short3(kf, 0, SUB, kt) * short3(vf, 0, SUB, vt)
    whole_ref[0:SUB] = head
    first = seam_ref[0] * head[0:1] + seam_ref[1] * head[1:2]
    for c in range(enter_ref.shape[0]):
        into_ref[c] = enter_ref[c] + first
        first = first * hop_ref[...]
    out_ref[...] = fresh_ref[...] + first


def merge_kernel(b, total_ref, got_ref, span_ref, out_ref):
    upper = (lax.axis_index("ctx") >> b) % 2 == 1
    total, got = total_ref[...], got_ref[...]
    late = jnp.where(upper, total, got)
    early = jnp.where(upper, got, total)
    out_ref[...] = late + span_ref[b] * early


def query_kernel(halo_ref, q_ref, sf_ref, out_ref, qf):
    length, width = q_ref.shape
    keep = jnp.where(lax.axis_index("ctx") > 0, 1.0, 0.0).astype(F32)
    for lane in range(0, width, LANES):
        at = slice(lane, lane + LANES)
        taps = [sf_ref[0, i : i + 1, at] for i in range(3)]
        qf[0:SUB] = halo_ref[0:RIM, at].astype(F32) * keep
        piece = 64
        for start in range(0, length, piece):
            rows = slice(start, start + piece)
            qf[SUB + start : SUB + start + piece] = q_ref[rows, at].astype(F32)
            out_ref[rows, at] = short3(qf, start, piece, taps)


def near_kernel(size, first, gated_ref, query_ref, into_ref, row_ref, plain_ref, lead_hi, lead_lo, out_ref):
    length, lanes = out_ref.shape
    modes = into_ref.shape[1]
    chunks = length // LANES
    groups = LANES // size
    down = lax.broadcasted_iota(jnp.int32, (LANES, LANES), 0)
    along = lax.broadcasted_iota(jnp.int32, (LANES, LANES), 1)
    causal = along >= down
    block = down // modes == along // size

    for tile in range(lanes // LANES):
        at = slice(first + tile * LANES, first + (tile + 1) * LANES)
        to = slice(tile * LANES, (tile + 1) * LANES)
        rate = jnp.transpose(jnp.broadcast_to(row_ref[0:1, at], (LANES, LANES)))
        gain = jnp.transpose(jnp.broadcast_to(row_ref[1:2, at], (LANES, LANES)))
        curve = gain * jnp.exp(-rate * along.astype(F32))
        halves = [split2(jnp.transpose(gated_ref[c * LANES : (c + 1) * LANES, at])) for c in range(chunks)]
        outs = []
        for g in range(groups):
            rows = slice(g * size, (g + 1) * size)
            taps = jnp.sum(curve[g * modes : (g + 1) * modes], axis=0, keepdims=True)
            toe = pltpu.roll(jnp.broadcast_to(taps, (LANES, LANES)), 0, 1, stride=1, stride_axis=0)
            hi, lo = split2(jnp.where(causal, toe, 0.0))
            xh = jnp.concatenate([h[rows] for h, _ in halves], 0)
            xl = jnp.concatenate([l[rows] for _, l in halves], 0)
            out = jnp.dot(jnp.concatenate([xh, xl], 1), jnp.concatenate([hi, hi], 0), preferred_element_type=F32)
            outs.append(out + jnp.dot(xh, lo, preferred_element_type=F32))
        lead = jnp.concatenate([lead_hi[0:LANES, at], lead_lo[0:LANES, at]], 1)
        for c in range(chunks):
            rows = slice(c * LANES, (c + 1) * LANES)
            near = jnp.transpose(jnp.concatenate([o[c * size : (c + 1) * size] for o in outs], 0))
            near = near + plain_ref[:, at] * gated_ref[rows, at]
            if c:
                wide = jnp.where(block, jnp.concatenate([into_ref[c - 1, :, at]] * groups, 0), 0.0)
                hi, lo = split2(wide)
                near = near + jnp.dot(lead, jnp.concatenate([hi, hi], 0), preferred_element_type=F32)
                near = near + jnp.dot(lead[:, :LANES], lo, preferred_element_type=F32)
            out_ref[rows, to] = query_ref[rows, at] * near


def mix_kernel(size, phases, parts, *refs):
    query_ref, reach_ref, lead_hi, lead_lo = refs[:4]
    gots = refs[4 : 4 + phases]
    nears = refs[4 + phases : 4 + phases + parts]
    out_ref, stage, sem = refs[4 + phases + parts :]
    _, width = query_ref.shape
    modes = reach_ref.shape[1]
    where = []
    for ref in nears:
        where += [(ref, c) for c in range(0, ref.shape[1], LANES)]
    span = min(WIDE, width)
    groups = span // size
    row = lax.broadcasted_iota(jnp.int32, (groups * modes, span), 0)
    col = lax.broadcasted_iota(jnp.int32, (groups * modes, span), 1)
    block = row // modes == col // size
    copies = []
    for tile in range(width // span):
        at = slice(tile * span, (tile + 1) * span)
        state = reach_ref[0, :, at] * gots[0][:, at]
        for b in range(1, phases):
            state = state + reach_ref[b, :, at] * gots[b][:, at]
        wide = jnp.where(block, jnp.concatenate([state] * groups, 0), 0.0)
        hi, lo = split2(wide)
        term = jnp.dot(lead_hi[:, at], hi, preferred_element_type=F32)
        term = term + jnp.dot(lead_lo[:, at], hi, preferred_element_type=F32)
        term = term + jnp.dot(lead_hi[:, at], lo, preferred_element_type=F32)
        for half in range(span // LANES):
            lane = tile * span + half * LANES
            cut = slice(lane, lane + LANES)
            near, c = where[lane // LANES]
            far = query_ref[:, cut] * term[:, half * LANES : (half + 1) * LANES]
            stage[:, cut] = (near[:, c : c + LANES] + far).astype(BF16)
        copy = pltpu.make_async_copy(stage.at[:, at], out_ref.at[:, at], sem.at[tile])
        copy.start()
        copies.append(copy)
    for copy in copies:
        copy.wait()


def body(query_in, key_in, value_in, residues, decay_rate, short_filter, skip_gain):
    length, width = query_in.shape
    modes, groups = residues.shape
    size = width // groups
    ranks = lax.axis_size("ctx")
    phases = ranks.bit_length() - 1
    rims = pl.pallas_call(
        rim_kernel,
        in_specs=[pl.BlockSpec(memory_space=pltpu.HBM)] * 3,
        out_specs=VMEM,
        out_shape=jax.ShapeDtypeStruct((3 * RIM, width), BF16),
        scratch_shapes=[pltpu.SemaphoreType.DMA((3,))],
        compiler_params=pltpu.CompilerParams(vmem_limit_bytes=4 << 20),
        name="rim",
    )(*[pltpu.with_memory_space_constraint(a, pltpu.HBM) for a in (query_in, key_in, value_in)])
    halo = lax.ppermute(rims, "ctx", [(i, (i + 1) % ranks) for i in range(ranks)])

    lead_shape = jax.ShapeDtypeStruct((length, width), BF16)
    tail_shape = jax.ShapeDtypeStruct((width, 2 * LANES), BF16)
    scan_shape = lambda count: jax.ShapeDtypeStruct((count, modes, width), F32)
    row_shape = jax.ShapeDtypeStruct((modes, width), F32)
    lead_hi, lead_lo, tail, row, plain, hop, seam, span, reach = pl.pallas_call(
        table_kernel,
        in_specs=[VMEM] * 3,
        out_specs=[VMEM] * 9,
        out_shape=[
            lead_shape,
            lead_shape,
            tail_shape,
            jax.ShapeDtypeStruct((2, width), F32),
            jax.ShapeDtypeStruct((1, width), F32),
            row_shape,
            scan_shape(2),
            scan_shape(max(1, phases - 1)),
            scan_shape(phases),
        ],
        compiler_params=PARAMS,
        cost_estimate=pl.CostEstimate(flops=10**7, bytes_accessed=5 << 20, transcendentals=0),
        name="tables",
    )(residues, decay_rate, skip_gain)

    tile = min(width, WIDE)
    cols = lambda rows: pl.BlockSpec((rows, tile), lambda j: (0, j))
    gated_shape = jax.ShapeDtypeStruct((length, width), F32)
    enter_shape = scan_shape(length // LANES - 1)
    gated, fresh, enter = pl.pallas_call(
        functools.partial(state_kernel, size),
        grid=(width // tile,),
        in_specs=[
            cols(length),
            cols(length),
            pl.BlockSpec((3, 3, tile), lambda j: (0, 0, j)),
            VMEM,
            VMEM,
        ],
        out_specs=[VMEM] * 3,
        out_shape=[gated_shape, row_shape, enter_shape],
        scratch_shapes=[pltpu.VMEM((SUB + length, LANES), F32)] * 2,
        compiler_params=PARAMS,
        cost_estimate=pl.CostEstimate(flops=10**7, bytes_accessed=5 << 20, transcendentals=0),
        name="state",
    )(key_in, value_in, short_filter, tail, hop)
    fresh, into, gated = pl.pallas_call(
        seam_kernel,
        in_specs=[VMEM] * 9,
        out_specs=[VMEM] * 3,
        out_shape=[row_shape, enter_shape, gated_shape],
        input_output_aliases={8: 2},
        scratch_shapes=[pltpu.VMEM((2 * SUB, width), F32)] * 2,
        compiler_params=PARAMS,
        name="seam",
    )(halo, key_in, value_in, short_filter, seam, hop, fresh, enter, gated)

    query = pl.pallas_call(
        query_kernel,
        in_specs=[VMEM] * 3,
        out_specs=VMEM,
        out_shape=gated_shape,
        scratch_shapes=[pltpu.VMEM((SUB + length, LANES), F32)],
        compiler_params=PARAMS,
        cost_estimate=pl.CostEstimate(flops=10**7, bytes_accessed=4 << 20, transcendentals=0),
        name="query",
    )(halo, query_in, short_filter)

    unit = LANES if width // LANES >= 2 * phases else min(width, WIDE)
    cuts = [width // unit * b // phases * unit for b in range(phases + 1)]
    nears, gots, total = [], [], fresh
    for b in range(phases):
        got = lax.ppermute(total, "ctx", [(i, i ^ (1 << b)) for i in range(ranks)])
        gots.append(got)
        lanes = cuts[b + 1] - cuts[b]
        if lanes:
            nears.append(
                pl.pallas_call(
                    functools.partial(near_kernel, size, cuts[b]),
                    in_specs=[VMEM] * 7,
                    out_specs=VMEM,
                    out_shape=jax.ShapeDtypeStruct((length, lanes), F32),
                    compiler_params=PARAMS,
                    cost_estimate=pl.CostEstimate(flops=10**7, bytes_accessed=4 << 20, transcendentals=0),
                    name="near",
                )(gated, query, into, row, plain, lead_hi, lead_lo)
            )
        if b + 1 < phases:
            total = pl.pallas_call(
                functools.partial(merge_kernel, b),
                in_specs=[VMEM] * 3,
                out_specs=VMEM,
                out_shape=row_shape,
                compiler_params=PARAMS,
                name="merge",
            )(total, got, span)

    return pl.pallas_call(
        functools.partial(mix_kernel, size, phases, len(nears)),
        in_specs=[VMEM] * (4 + phases + len(nears)),
        out_specs=pl.BlockSpec(memory_space=pl.ANY),
        out_shape=jax.ShapeDtypeStruct((length, width), BF16),
        scratch_shapes=[
            pltpu.VMEM((length, width), BF16),
            pltpu.SemaphoreType.DMA((max(1, width // WIDE),)),
        ],
        compiler_params=PARAMS,
        name="mix",
    )(query, reach, lead_hi, lead_lo, *gots, *nears)


def solution(mesh):
    placed = (
        P("ctx", "fsdp"),
        P("ctx", "fsdp"),
        P("ctx", "fsdp"),
        P(None, "fsdp"),
        P(None, "fsdp"),
        P(None, None, "fsdp"),
        P(None, "fsdp"),
    )
    return jax.shard_map(body, mesh=mesh, in_specs=placed, out_specs=P("ctx", "fsdp"), check_vma=False)
```

```python
import functools

import jax
import jax.numpy as jnp
from jax import lax
from jax.experimental import pallas as pl
from jax.experimental.pallas import tpu as pltpu
from jax.sharding import PartitionSpec as P


LANES = 128
WIDE = 256
SUB = 8
RIM = 8
F32 = jnp.float32
BF16 = jnp.bfloat16
VMEM = pl.BlockSpec(memory_space=pltpu.VMEM)
PARAMS = pltpu.CompilerParams(vmem_limit_bytes=8 << 20)


def split2(x):
    hi = x.astype(BF16)
    return hi, (x - hi.astype(F32)).astype(BF16)


def expand(table, first, lanes, size):
    groups = table.shape[1]
    row = lax.broadcasted_iota(jnp.int32, (groups, lanes), 0)
    col = lax.broadcasted_iota(jnp.int32, (groups, lanes), 1)
    pick = (row == first + col // size).astype(BF16)
    one, _ = split2(table)
    two, three = split2(table - one.astype(F32))
    out = jnp.dot(one, pick, preferred_element_type=F32)
    out = out + jnp.dot(two, pick, preferred_element_type=F32)
    return out + jnp.dot(three, pick, preferred_element_type=F32)


def norm_of(decay):
    x = 2.0 * decay
    total = jnp.full_like(x, 1.0)
    for k in range(9, 1, -1):
        total = 1.0 - x * total * (1.0 / k)
    return jnp.sqrt(x * total)


def short3(ref, start, count, taps):
    at = SUB + start
    out = taps[0] * ref[at : at + count]
    out = out + taps[1] * ref[at - 1 : at - 1 + count]
    return out + taps[2] * ref[at - 2 : at - 2 + count]


def rim_kernel(q_ref, k_ref, v_ref, out_ref, sem):
    copies = []
    for i, ref in enumerate((q_ref, k_ref, v_ref)):
        rim = ref.at[ref.shape[0] - RIM :]
        copies.append(pltpu.make_async_copy(rim, out_ref.at[i * RIM : (i + 1) * RIM], sem.at[i]))
        copies[i].start()
    for copy in copies:
        copy.wait()


def steps_of(ranks):
    bits = ranks.bit_length() - 1
    return [(low, min(2, bits - low)) for low in range(0, bits, 2)]


def gaps_of(ranks, length):
    me = lax.axis_index("ctx")
    table = []
    for low, count in steps_of(ranks):
        mine = (me >> low) % (1 << count)
        inner = me % (1 << low) * length
        size = length << low
        row = []
        for m in range(1 << count):
            other = mine ^ m
            reach = size * (mine - 1 - other) + inner
            after = size * ((1 << count) - 1 - other)
            row.append((other < mine, jnp.maximum(reach, 0).astype(F32), after.astype(F32)))
        table.append(row)
    return table


def table_kernel(ranks, res_ref, decay_ref, skip_ref, lead_hi, lead_lo, tail_ref, row_ref, plain_ref, hop_ref, seam_ref, span_ref, reach_ref):
    length, width = lead_hi.shape
    modes = decay_ref.shape[0]
    gaps = gaps_of(ranks, length)
    plain_ref[...] = skip_ref[...]
    lane = lax.broadcasted_iota(jnp.int32, (modes, LANES), 1)
    own = lane % modes == lax.broadcasted_iota(jnp.int32, (modes, LANES), 0)
    down = lax.broadcasted_iota(jnp.int32, (LANES, LANES), 0).astype(F32)
    along = lax.broadcasted_iota(jnp.int32, (LANES, LANES), 1).astype(F32)
    for tile in range(width // LANES):
        at = slice(tile * LANES, (tile + 1) * LANES)
        rates = expand(decay_ref[...], tile * (LANES // modes), LANES, modes)
        gains = expand(res_ref[...], tile * (LANES // modes), LANES, modes) * norm_of(rates)
        rate = jnp.sum(jnp.where(own, rates, 0.0), axis=0, keepdims=True)
        gain = jnp.sum(jnp.where(own, gains, 0.0), axis=0, keepdims=True)
        row_ref[0:1, at] = rate
        row_ref[1:2, at] = gain
        hop_ref[:, at] = jnp.exp(-rates * float(LANES))
        for i in range(2):
            seam_ref[i, :, at] = jnp.exp(-rates * (LANES - 1.0 - i))
        e = f = 0
        for step, row in enumerate(gaps):
            for m, (before, gap, after) in enumerate(row):
                if m:
                    reach_ref[e, :, at] = jnp.where(before, jnp.exp(-rates * gap), 0.0)
                    e += 1
                if step + 1 < len(gaps):
                    span_ref[f, :, at] = jnp.exp(-rates * after)
                    f += 1
        rate_rows = jnp.transpose(jnp.broadcast_to(rate, (LANES, LANES)))
        tail_ref[at, 0:LANES], tail_ref[at, LANES:] = split2(jnp.exp(-rate_rows * (LANES - 1.0 - along)))
        lead = gain * jnp.exp(-rate * (down + 1.0))
        hop = jnp.exp(-rate * float(LANES))
        for c in range(length // LANES):
            rows = slice(c * LANES, (c + 1) * LANES)
            lead_hi[rows, at], lead_lo[rows, at] = split2(lead)
            lead = lead * hop


def state_kernel(size, k_ref, v_ref, sf_ref, tail_ref, hop_ref, q_ref, gated_ref, fresh_ref, enter_ref, kf, vf):
    length, lanes = k_ref.shape
    modes = fresh_ref.shape[0]
    tile = pl.program_id(0)
    row = lax.broadcasted_iota(jnp.int32, (modes, LANES), 1) // size
    piece = 64
    inner = lax.broadcasted_iota(jnp.int32, (piece, LANES), 0) >= 2
    kf[0:SUB] = jnp.zeros((SUB, LANES), F32)
    vf[0:SUB] = jnp.zeros((SUB, LANES), F32)
    for part in range(lanes // LANES):
        at = slice(part * LANES, (part + 1) * LANES)
        base = pl.multiple_of(tile * lanes + part * LANES, LANES)
        own = pl.ds(base, LANES)
        kt = [sf_ref[1, i : i + 1, at] for i in range(3)]
        vt = [sf_ref[2, i : i + 1, at] for i in range(3)]
        hop = hop_ref[:, own]
        tail, tail_hi = tail_ref[own, :], tail_ref[own, 0:LANES]
        total = jnp.zeros((modes, LANES), F32)
        for c in range(length // LANES):
            his, los = [], []
            for start in range(c * LANES, (c + 1) * LANES, piece):
                rows = slice(start, start + piece)
                kf[SUB + start : SUB + start + piece] = k_ref[rows, at].astype(F32)
                vf[SUB + start : SUB + start + piece] = v_ref[rows, at].astype(F32)
                gated = short3(kf, start, piece, kt) * short3(vf, start, piece, vt)
                if start == 0:
                    gated = jnp.where(inner, gated, 0.0)
                gated_ref[rows, own] = gated
                hi, lo = split2(gated)
                his.append(hi)
                los.append(lo)
            out = jnp.dot(tail, jnp.concatenate(his + his, 0), preferred_element_type=F32)
            out = out + jnp.dot(tail_hi, jnp.concatenate(los, 0), preferred_element_type=F32)
            fresh = jnp.zeros((modes, LANES), F32)
            for g in range(LANES // size):
                fresh = jnp.where(row == g, out[g * modes : (g + 1) * modes], fresh)
            if c:
                enter_ref[c - 1, :, own] = total
            total = total * hop + fresh
        fresh_ref[:, own] = total


def seam_kernel(halo_ref, k_ref, v_ref, sf_ref, seam_ref, hop_ref, fresh_ref, enter_ref, gated_ref, out_ref, into_ref, whole_ref, kf, vf):
    keep = jnp.where(lax.axis_index("ctx") > 0, 1.0, 0.0).astype(F32)
    kf[0:SUB] = halo_ref[RIM : 2 * RIM].astype(F32) * keep
    vf[0:SUB] = halo_ref[2 * RIM : 3 * RIM].astype(F32) * keep
    kf[SUB:] = k_ref[0:SUB].astype(F32)
    vf[SUB:] = v_ref[0:SUB].astype(F32)
    kt = [sf_ref[1, i : i + 1, :] for i in range(3)]
    vt = [sf_ref[2, i : i + 1, :] for i in range(3)]
    head = short3(kf, 0, SUB, kt) * short3(vf, 0, SUB, vt)
    whole_ref[0:SUB] = head
    first = seam_ref[0] * head[0:1] + seam_ref[1] * head[1:2]
    for c in range(enter_ref.shape[0]):
        into_ref[c] = enter_ref[c] + first
        first = first * hop_ref[...]
    out_ref[...] = fresh_ref[...] + first


def merge_kernel(first, at, *refs):
    span_ref, reach_ref, total_ref, next_ref = refs[-4:]
    got = refs[1 : -4 if first == 0 else -5]
    total = span_ref[at] * refs[0][...]
    prefix = 0.0 if first == 0 else refs[-5][...]
    for m, ref in enumerate(got):
        value = ref[...]
        total = total + span_ref[at + 1 + m] * value
        prefix = prefix + reach_ref[first + m] * value
    total_ref[...] = total
    next_ref[...] = prefix


def query_kernel(halo_ref, q_ref, sf_ref, out_ref, qf):
    length, width = q_ref.shape
    keep = jnp.where(lax.axis_index("ctx") > 0, 1.0, 0.0).astype(F32)
    for lane in range(0, width, LANES):
        at = slice(lane, lane + LANES)
        taps = [sf_ref[0, i : i + 1, at] for i in range(3)]
        qf[0:SUB] = halo_ref[0:RIM, at].astype(F32) * keep
        piece = 64
        for start in range(0, length, piece):
            rows = slice(start, start + piece)
            qf[SUB + start : SUB + start + piece] = q_ref[rows, at].astype(F32)
            out_ref[rows, at] = short3(qf, start, piece, taps)


def near_kernel(size, first, gated_ref, query_ref, into_ref, row_ref, plain_ref, lead_hi, lead_lo, out_ref):
    length, lanes = out_ref.shape
    modes = into_ref.shape[1]
    chunks = length // LANES
    groups = LANES // size
    down = lax.broadcasted_iota(jnp.int32, (LANES, LANES), 0)
    along = lax.broadcasted_iota(jnp.int32, (LANES, LANES), 1)
    causal = along >= down
    block = down // modes == along // size

    for tile in range(lanes // LANES):
        at = slice(first + tile * LANES, first + (tile + 1) * LANES)
        to = slice(tile * LANES, (tile + 1) * LANES)
        rate = jnp.transpose(jnp.broadcast_to(row_ref[0:1, at], (LANES, LANES)))
        gain = jnp.transpose(jnp.broadcast_to(row_ref[1:2, at], (LANES, LANES)))
        curve = gain * jnp.exp(-rate * along.astype(F32))
        halves = [split2(jnp.transpose(gated_ref[c * LANES : (c + 1) * LANES, at])) for c in range(chunks)]
        outs = []
        for g in range(groups):
            rows = slice(g * size, (g + 1) * size)
            taps = jnp.sum(curve[g * modes : (g + 1) * modes], axis=0, keepdims=True)
            toe = pltpu.roll(jnp.broadcast_to(taps, (LANES, LANES)), 0, 1, stride=1, stride_axis=0)
            hi, lo = split2(jnp.where(causal, toe, 0.0))
            xh = jnp.concatenate([h[rows] for h, _ in halves], 0)
            xl = jnp.concatenate([l[rows] for _, l in halves], 0)
            out = jnp.dot(jnp.concatenate([xh, xl], 1), jnp.concatenate([hi, hi], 0), preferred_element_type=F32)
            outs.append(out + jnp.dot(xh, lo, preferred_element_type=F32))
        lead = jnp.concatenate([lead_hi[0:LANES, at], lead_lo[0:LANES, at]], 1)
        for c in range(chunks):
            rows = slice(c * LANES, (c + 1) * LANES)
            near = jnp.transpose(jnp.concatenate([o[c * size : (c + 1) * size] for o in outs], 0))
            near = near + plain_ref[:, at] * gated_ref[rows, at]
            if c:
                wide = jnp.where(block, jnp.concatenate([into_ref[c - 1, :, at]] * groups, 0), 0.0)
                hi, lo = split2(wide)
                near = near + jnp.dot(lead, jnp.concatenate([hi, hi], 0), preferred_element_type=F32)
                near = near + jnp.dot(lead[:, :LANES], lo, preferred_element_type=F32)
            out_ref[rows, to] = query_ref[rows, at] * near


def mix_kernel(size, first, count, parts, *refs):
    query_ref, reach_ref, lead_hi, lead_lo = refs[:4]
    gots = refs[4 : 4 + count]
    nears = refs[4 + count : 4 + count + parts]
    prefix = refs[4 + count + parts : -3]
    out_ref, stage, sem = refs[-3:]
    _, width = query_ref.shape
    modes = reach_ref.shape[1]
    where = []
    for ref in nears:
        where += [(ref, c) for c in range(0, ref.shape[1], LANES)]
    span = min(WIDE, width)
    groups = span // size
    row = lax.broadcasted_iota(jnp.int32, (groups * modes, span), 0)
    col = lax.broadcasted_iota(jnp.int32, (groups * modes, span), 1)
    block = row // modes == col // size
    copies = []
    for tile in range(width // span):
        at = slice(tile * span, (tile + 1) * span)
        state = prefix[0][:, at] if prefix else 0.0
        for m in range(count):
            state = state + reach_ref[first + m, :, at] * gots[m][:, at]
        wide = jnp.where(block, jnp.concatenate([state] * groups, 0), 0.0)
        hi, lo = split2(wide)
        term = jnp.dot(lead_hi[:, at], hi, preferred_element_type=F32)
        term = term + jnp.dot(lead_lo[:, at], hi, preferred_element_type=F32)
        term = term + jnp.dot(lead_hi[:, at], lo, preferred_element_type=F32)
        for half in range(span // LANES):
            lane = tile * span + half * LANES
            cut = slice(lane, lane + LANES)
            near, c = where[lane // LANES]
            far = query_ref[:, cut] * term[:, half * LANES : (half + 1) * LANES]
            stage[:, cut] = (near[:, c : c + LANES] + far).astype(BF16)
        copy = pltpu.make_async_copy(stage.at[:, at], out_ref.at[:, at], sem.at[tile])
        copy.start()
        copies.append(copy)
    for copy in copies:
        copy.wait()


def body(query_in, key_in, value_in, residues, decay_rate, short_filter, skip_gain):
    length, width = query_in.shape
    modes, groups = residues.shape
    size = width // groups
    ranks = lax.axis_size("ctx")
    steps = steps_of(ranks)
    reaches = sum((1 << count) - 1 for _, count in steps)
    spans = sum(1 << count for _, count in steps[:-1])
    rims = pl.pallas_call(
        rim_kernel,
        in_specs=[pl.BlockSpec(memory_space=pltpu.HBM)] * 3,
        out_specs=VMEM,
        out_shape=jax.ShapeDtypeStruct((3 * RIM, width), BF16),
        scratch_shapes=[pltpu.SemaphoreType.DMA((3,))],
        compiler_params=pltpu.CompilerParams(vmem_limit_bytes=4 << 20),
        name="rim",
    )(*[pltpu.with_memory_space_constraint(a, pltpu.HBM) for a in (query_in, key_in, value_in)])
    halo = lax.ppermute(rims, "ctx", [(i, (i + 1) % ranks) for i in range(ranks)])

    lead_shape = jax.ShapeDtypeStruct((length, width), BF16)
    tail_shape = jax.ShapeDtypeStruct((width, 2 * LANES), BF16)
    scan_shape = lambda count: jax.ShapeDtypeStruct((count, modes, width), F32)
    row_shape = jax.ShapeDtypeStruct((modes, width), F32)
    lead_hi, lead_lo, tail, row, plain, hop, seam, span, reach = pl.pallas_call(
        functools.partial(table_kernel, ranks),
        in_specs=[VMEM] * 3,
        out_specs=[VMEM] * 9,
        out_shape=[
            lead_shape,
            lead_shape,
            tail_shape,
            jax.ShapeDtypeStruct((2, width), F32),
            jax.ShapeDtypeStruct((1, width), F32),
            row_shape,
            scan_shape(2),
            scan_shape(max(1, spans)),
            scan_shape(reaches),
        ],
        compiler_params=PARAMS,
        cost_estimate=pl.CostEstimate(flops=10**7, bytes_accessed=5 << 20, transcendentals=0),
        name="tables",
    )(residues, decay_rate, skip_gain)

    tile = min(width, WIDE)
    cols = lambda rows: pl.BlockSpec((rows, tile), lambda j: (0, j))
    gated_shape = jax.ShapeDtypeStruct((length, width), F32)
    enter_shape = scan_shape(length // LANES - 1)
    gated, fresh, enter = pl.pallas_call(
        functools.partial(state_kernel, size),
        grid=(width // tile,),
        in_specs=[
            cols(length),
            cols(length),
            pl.BlockSpec((3, 3, tile), lambda j: (0, 0, j)),
            VMEM,
            VMEM,
            VMEM,
        ],
        out_specs=[VMEM] * 3,
        out_shape=[gated_shape, row_shape, enter_shape],
        scratch_shapes=[pltpu.VMEM((SUB + length, LANES), F32)] * 2,
        compiler_params=PARAMS,
        cost_estimate=pl.CostEstimate(flops=10**7, bytes_accessed=5 << 20, transcendentals=0),
        name="state",
    )(key_in, value_in, short_filter, tail, hop, query_in)
    fresh, into, gated = pl.pallas_call(
        seam_kernel,
        in_specs=[VMEM] * 9,
        out_specs=[VMEM] * 3,
        out_shape=[row_shape, enter_shape, gated_shape],
        input_output_aliases={8: 2},
        scratch_shapes=[pltpu.VMEM((2 * SUB, width), F32)] * 2,
        compiler_params=PARAMS,
        name="seam",
    )(halo, key_in, value_in, short_filter, seam, hop, fresh, enter, gated)

    query = pl.pallas_call(
        query_kernel,
        in_specs=[VMEM] * 3,
        out_specs=VMEM,
        out_shape=gated_shape,
        scratch_shapes=[pltpu.VMEM((SUB + length, LANES), F32)],
        compiler_params=PARAMS,
        cost_estimate=pl.CostEstimate(flops=10**7, bytes_accessed=4 << 20, transcendentals=0),
        name="query",
    )(halo, query_in, short_filter)

    cuts = [width // LANES * b // len(steps) * LANES for b in range(len(steps) + 1)]
    nears, total, prefix, first, at = [], fresh, [], 0, 0
    for b, (low, count) in enumerate(steps):
        gots = []
        for m in range(1, 1 << count):
            gots.append(lax.ppermute(total, "ctx", [(i, i ^ (m << low)) for i in range(ranks)]))
        lanes = cuts[b + 1] - cuts[b]
        if lanes:
            nears.append(
                pl.pallas_call(
                    functools.partial(near_kernel, size, cuts[b]),
                    in_specs=[VMEM] * 7,
                    out_specs=VMEM,
                    out_shape=jax.ShapeDtypeStruct((length, lanes), F32),
                    compiler_params=PARAMS,
                    cost_estimate=pl.CostEstimate(flops=10**7, bytes_accessed=4 << 20, transcendentals=0),
                    name="near",
                )(gated, query, into, row, plain, lead_hi, lead_lo)
            )
        if b + 1 < len(steps):
            total, ahead = pl.pallas_call(
                functools.partial(merge_kernel, first, at),
                in_specs=[VMEM] * (3 + len(gots) + len(prefix)),
                out_specs=[VMEM] * 2,
                out_shape=[row_shape] * 2,
                compiler_params=PARAMS,
                name="merge",
            )(total, *gots, *prefix, span, reach)
            prefix = [ahead]
            first += len(gots)
            at += 1 << count

    return pl.pallas_call(
        functools.partial(mix_kernel, size, first, len(gots), len(nears)),
        in_specs=[VMEM] * (4 + len(gots) + len(nears) + len(prefix)),
        out_specs=pl.BlockSpec(memory_space=pl.ANY),
        out_shape=jax.ShapeDtypeStruct((length, width), BF16),
        scratch_shapes=[
            pltpu.VMEM((length, width), BF16),
            pltpu.SemaphoreType.DMA((max(1, width // WIDE),)),
        ],
        compiler_params=PARAMS,
        name="mix",
    )(query, reach, lead_hi, lead_lo, *gots, *nears, *prefix)


def solution(mesh):
    placed = (
        P("ctx", "fsdp"),
        P("ctx", "fsdp"),
        P("ctx", "fsdp"),
        P(None, "fsdp"),
        P(None, "fsdp"),
        P(None, None, "fsdp"),
        P(None, "fsdp"),
    )
    return jax.shard_map(body, mesh=mesh, in_specs=placed, out_specs=P("ctx", "fsdp"), check_vma=False)
```

```python
import functools

import jax
import jax.numpy as jnp
from jax import lax
from jax.experimental import pallas as pl
from jax.experimental.pallas import tpu as pltpu
from jax.sharding import PartitionSpec as P


LANES = 128
WIDE = 256
SUB = 8
F32 = jnp.float32
BF16 = jnp.bfloat16
VMEM = pl.BlockSpec(memory_space=pltpu.VMEM)
PARAMS = pltpu.CompilerParams(vmem_limit_bytes=8 << 20)


def split2(x):
    hi = x.astype(BF16)
    return hi, (x - hi.astype(F32)).astype(BF16)


def pair(hi, lo):
    return jnp.concatenate([jnp.concatenate([hi, lo], 1), jnp.concatenate([hi, jnp.zeros_like(lo)], 1)], 0)


def dot3(left, right):
    out = jnp.dot(left, right, preferred_element_type=F32)
    return out[:, :LANES] + out[:, LANES:]


def expand(table, first, lanes, size):
    groups = table.shape[1]
    row = lax.broadcasted_iota(jnp.int32, (groups, lanes), 0)
    col = lax.broadcasted_iota(jnp.int32, (groups, lanes), 1)
    pick = (row == first + col // size).astype(BF16)
    one, _ = split2(table)
    two, three = split2(table - one.astype(F32))
    out = jnp.dot(one, pick, preferred_element_type=F32)
    out = out + jnp.dot(two, pick, preferred_element_type=F32)
    return out + jnp.dot(three, pick, preferred_element_type=F32)


def norm_of(decay):
    x = 2.0 * decay
    total = jnp.full_like(x, 1.0)
    for k in range(9, 1, -1):
        total = 1.0 - x * total * (1.0 / k)
    return jnp.sqrt(x * total)


def short3(ref, start, count, taps):
    at = SUB + start
    out = taps[0] * ref[at : at + count]
    out = out + taps[1] * ref[at - 1 : at - 1 + count]
    return out + taps[2] * ref[at - 2 : at - 2 + count]


def rim_kernel(q_ref, k_ref, v_ref, *refs):
    small, out_ref, loaded, rows, sem = refs[:3], refs[3], refs[4:7], refs[7], refs[8]
    pairs = [(ref.at[ref.shape[0] - SUB :], rows.at[i]) for i, ref in enumerate((q_ref, k_ref, v_ref))]
    pairs += list(zip(small, loaded))
    copies = [pltpu.make_async_copy(src, dst, sem.at[i]) for i, (src, dst) in enumerate(pairs)]
    for copy in copies:
        copy.start()
    for copy in copies:
        copy.wait()
    ends = [rows[i].astype(F32)[SUB - 2 :] for i in range(3)]
    out_ref[...] = jnp.concatenate(ends + ends[:1], 0).astype(BF16)


def past(halo_ref, which, at=slice(None)):
    keep = jnp.where(lax.axis_index("ctx") > 0, 1.0, 0.0).astype(F32)
    return halo_ref[:, at].astype(F32)[2 * which : 2 * which + 2] * keep


def steps_of(ranks):
    bits = ranks.bit_length() - 1
    return [(low, min(2, bits - low)) for low in range(0, bits, 2)]


def gaps_of(ranks, length):
    me = lax.axis_index("ctx")
    table = []
    for low, count in steps_of(ranks):
        mine = (me >> low) % (1 << count)
        inner = me % (1 << low) * length
        size = length << low
        row = []
        for m in range(1 << count):
            other = mine ^ m
            reach = size * (mine - 1 - other) + inner
            after = size * ((1 << count) - 1 - other)
            row.append((other < mine, jnp.maximum(reach, 0).astype(F32), after.astype(F32)))
        table.append(row)
    return table


def table_kernel(ranks, res_ref, decay_ref, skip_ref, lead_ref, tail_ref, row_ref, plain_ref, hop_ref, seam_ref, span_ref, reach_ref):
    length, width = lead_ref.shape[0], skip_ref.shape[1]
    modes = decay_ref.shape[0]
    gaps = gaps_of(ranks, length)
    plain_ref[...] = skip_ref[...]
    lane = lax.broadcasted_iota(jnp.int32, (modes, LANES), 1)
    own = lane % modes == lax.broadcasted_iota(jnp.int32, (modes, LANES), 0)
    down = lax.broadcasted_iota(jnp.int32, (LANES, LANES), 0).astype(F32)
    along = lax.broadcasted_iota(jnp.int32, (LANES, LANES), 1).astype(F32)
    for tile in range(width // LANES):
        at = slice(tile * LANES, (tile + 1) * LANES)
        rates = expand(decay_ref[...], tile * (LANES // modes), LANES, modes)
        gains = expand(res_ref[...], tile * (LANES // modes), LANES, modes) * norm_of(rates)
        rate = jnp.sum(jnp.where(own, rates, 0.0), axis=0, keepdims=True)
        gain = jnp.sum(jnp.where(own, gains, 0.0), axis=0, keepdims=True)
        row_ref[0:1, at] = rate
        row_ref[1:2, at] = gain
        hop_ref[:, at] = jnp.exp(-rates * float(LANES))
        for i in range(2):
            seam_ref[i, :, at] = jnp.exp(-rates * (LANES - 1.0 - i))
        e = f = 0
        for step, row in enumerate(gaps):
            for m, (before, gap, after) in enumerate(row):
                if m:
                    reach_ref[e, :, at] = jnp.where(before, jnp.exp(-rates * gap), 0.0)
                    e += 1
                if step + 1 < len(gaps):
                    span_ref[f, :, at] = jnp.exp(-rates * after)
                    f += 1
        rate_rows = jnp.transpose(jnp.broadcast_to(rate, (LANES, LANES)))
        tail_ref[at, 0:LANES], tail_ref[at, LANES:] = split2(jnp.exp(-rate_rows * (LANES - 1.0 - along)))
        lead = gain * jnp.exp(-rate * (down + 1.0))
        hop = jnp.exp(-rate * float(LANES))
        for c in range(length // LANES):
            rows = slice(c * LANES, (c + 1) * LANES)
            mid = 2 * tile * LANES + LANES
            lead_ref[rows, mid - LANES : mid], lead_ref[rows, mid : mid + LANES] = split2(lead)
            lead = lead * hop


def state_kernel(size, k_ref, v_ref, sf_ref, tail_ref, hop_ref, q_ref, gated_ref, fresh_ref, enter_ref, kf, vf):
    length, lanes = k_ref.shape
    modes = fresh_ref.shape[0]
    tile = pl.program_id(0)
    row = lax.broadcasted_iota(jnp.int32, (modes, LANES), 1) // size
    piece = 64
    inner = lax.broadcasted_iota(jnp.int32, (piece, LANES), 0) >= 2
    kf[0:SUB] = jnp.zeros((SUB, LANES), F32)
    vf[0:SUB] = jnp.zeros((SUB, LANES), F32)
    for part in range(lanes // LANES):
        at = slice(part * LANES, (part + 1) * LANES)
        base = pl.multiple_of(tile * lanes + part * LANES, LANES)
        own = pl.ds(base, LANES)
        kt = [sf_ref[1, i : i + 1, at] for i in range(3)]
        vt = [sf_ref[2, i : i + 1, at] for i in range(3)]
        hop = hop_ref[:, own]
        tail = tail_ref[own, :]
        total = jnp.zeros((modes, LANES), F32)
        for c in range(length // LANES):
            his, los = [], []
            for start in range(c * LANES, (c + 1) * LANES, piece):
                rows = slice(start, start + piece)
                kf[SUB + start : SUB + start + piece] = k_ref[rows, at].astype(F32)
                vf[SUB + start : SUB + start + piece] = v_ref[rows, at].astype(F32)
                gated = short3(kf, start, piece, kt) * short3(vf, start, piece, vt)
                if start == 0:
                    gated = jnp.where(inner, gated, 0.0)
                gated_ref[rows, own] = gated
                hi, lo = split2(gated)
                his.append(hi)
                los.append(lo)
            out = dot3(tail, pair(jnp.concatenate(his, 0), jnp.concatenate(los, 0)))
            fresh = jnp.zeros((modes, LANES), F32)
            for g in range(LANES // size):
                fresh = jnp.where(row == g, out[g * modes : (g + 1) * modes], fresh)
            if c:
                enter_ref[c - 1, :, own] = total
            total = total * hop + fresh
        fresh_ref[:, own] = total


def seam_kernel(halo_ref, k_ref, v_ref, sf_ref, seam_ref, hop_ref, fresh_ref, enter_ref, gated_ref, out_ref, into_ref, whole_ref, kf, vf):
    kf[SUB - 2 : SUB] = past(halo_ref, 1)
    vf[SUB - 2 : SUB] = past(halo_ref, 2)
    kf[SUB:] = k_ref[0:SUB].astype(F32)
    vf[SUB:] = v_ref[0:SUB].astype(F32)
    kt = [sf_ref[1, i : i + 1, :] for i in range(3)]
    vt = [sf_ref[2, i : i + 1, :] for i in range(3)]
    head = short3(kf, 0, SUB, kt) * short3(vf, 0, SUB, vt)
    whole_ref[0:SUB] = head
    first = seam_ref[0] * head[0:1] + seam_ref[1] * head[1:2]
    for c in range(enter_ref.shape[0]):
        into_ref[c] = enter_ref[c] + first
        first = first * hop_ref[...]
    out_ref[...] = fresh_ref[...] + first


def merge_kernel(first, at, *refs):
    span_ref, reach_ref, total_ref, next_ref = refs[-4:]
    got = refs[1 : -4 if first == 0 else -5]
    total = span_ref[at] * refs[0][...]
    prefix = 0.0 if first == 0 else refs[-5][...]
    for m, ref in enumerate(got):
        value = ref[...]
        total = total + span_ref[at + 1 + m] * value
        prefix = prefix + reach_ref[first + m] * value
    total_ref[...] = total
    next_ref[...] = prefix


def query_kernel(halo_ref, q_ref, sf_ref, out_ref, qf):
    length, width = q_ref.shape
    for lane in range(0, width, LANES):
        at = slice(lane, lane + LANES)
        taps = [sf_ref[0, i : i + 1, at] for i in range(3)]
        qf[SUB - 2 : SUB] = past(halo_ref, 0, at)
        piece = 64
        for start in range(0, length, piece):
            rows = slice(start, start + piece)
            qf[SUB + start : SUB + start + piece] = q_ref[rows, at].astype(F32)
            out_ref[rows, at] = short3(qf, start, piece, taps)


def near_kernel(size, first, gated_ref, query_ref, into_ref, row_ref, plain_ref, lead_ref, out_ref):
    length, lanes = out_ref.shape
    modes = into_ref.shape[1]
    chunks = length // LANES
    groups = LANES // size
    down = lax.broadcasted_iota(jnp.int32, (LANES, LANES), 0)
    along = lax.broadcasted_iota(jnp.int32, (LANES, LANES), 1)
    causal = along >= down
    block = down // modes == along // size

    for tile in range(lanes // LANES):
        at = slice(first + tile * LANES, first + (tile + 1) * LANES)
        to = slice(tile * LANES, (tile + 1) * LANES)
        rate = jnp.transpose(jnp.broadcast_to(row_ref[0:1, at], (LANES, LANES)))
        gain = jnp.transpose(jnp.broadcast_to(row_ref[1:2, at], (LANES, LANES)))
        curve = gain * jnp.exp(-rate * along.astype(F32))
        halves = [split2(jnp.transpose(gated_ref[c * LANES : (c + 1) * LANES, at])) for c in range(chunks)]
        outs = []
        for g in range(groups):
            rows = slice(g * size, (g + 1) * size)
            taps = jnp.sum(curve[g * modes : (g + 1) * modes], axis=0, keepdims=True)
            toe = pltpu.roll(jnp.broadcast_to(taps, (LANES, LANES)), 0, 1, stride=1, stride_axis=0)
            hi, lo = split2(jnp.where(causal, toe, 0.0))
            xh = jnp.concatenate([h[rows] for h, _ in halves], 0)
            xl = jnp.concatenate([l[rows] for _, l in halves], 0)
            outs.append(dot3(jnp.concatenate([xh, xl], 1), pair(hi, lo)))
        lead = lead_ref[0:LANES, 2 * at.start : 2 * at.stop]
        for c in range(chunks):
            rows = slice(c * LANES, (c + 1) * LANES)
            near = jnp.transpose(jnp.concatenate([o[c * size : (c + 1) * size] for o in outs], 0))
            near = near + plain_ref[:, at] * gated_ref[rows, at]
            if c:
                wide = jnp.where(block, jnp.concatenate([into_ref[c - 1, :, at]] * groups, 0), 0.0)
                near = near + dot3(lead, pair(*split2(wide)))
            out_ref[rows, to] = query_ref[rows, at] * near


def mix_kernel(size, first, count, parts, *refs):
    query_ref, reach_ref, lead_ref = refs[:3]
    gots = refs[3 : 3 + count]
    nears = refs[3 + count : 3 + count + parts]
    prefix = refs[3 + count + parts : -3]
    out_ref, stage, sem = refs[-3:]
    length, width = query_ref.shape
    modes = reach_ref.shape[1]
    where = []
    for ref in nears:
        where += [(ref, c) for c in range(0, ref.shape[1], LANES)]
    groups = LANES // size
    row = lax.broadcasted_iota(jnp.int32, (groups * modes, LANES), 0)
    col = lax.broadcasted_iota(jnp.int32, (groups * modes, LANES), 1)
    block = row // modes == col // size
    copies = []
    for tile in range(width // LANES):
        at = slice(tile * LANES, (tile + 1) * LANES)
        state = prefix[0][:, at] if prefix else 0.0
        for m in range(count):
            state = state + reach_ref[first + m, :, at] * gots[m][:, at]
        wide = jnp.where(block, jnp.concatenate([state] * groups, 0), 0.0)
        right = pair(*split2(wide))
        near, c = where[tile]
        for start in range(0, length, LANES):
            rows = slice(start, start + LANES)
            term = dot3(lead_ref[rows, 2 * at.start : 2 * at.stop], right)
            stage[rows, at] = (near[rows, c : c + LANES] + query_ref[rows, at] * term).astype(BF16)
        copy = pltpu.make_async_copy(stage.at[:, at], out_ref.at[:, at], sem.at[tile])
        copy.start()
        copies.append(copy)
    for copy in copies:
        copy.wait()


def body(query_in, key_in, value_in, residues, decay_rate, short_filter, skip_gain):
    length, width = query_in.shape
    modes, groups = residues.shape
    size = width // groups
    ranks = lax.axis_size("ctx")
    steps = steps_of(ranks)
    reaches = sum((1 << count) - 1 for _, count in steps)
    spans = sum(1 << count for _, count in steps[:-1])
    small = (residues, decay_rate, skip_gain)
    sources = [pltpu.with_memory_space_constraint(a, pltpu.HBM) for a in (query_in, key_in, value_in) + small]
    rims, residues, decay_rate, skip_gain = pl.pallas_call(
        rim_kernel,
        in_specs=[pl.BlockSpec(memory_space=pltpu.HBM)] * 6,
        out_specs=[VMEM] * 4,
        out_shape=[jax.ShapeDtypeStruct((SUB, width), BF16)] + [jax.ShapeDtypeStruct(a.shape, F32) for a in small],
        scratch_shapes=[pltpu.VMEM((3, SUB, width), BF16), pltpu.SemaphoreType.DMA((6,))],
        compiler_params=PARAMS,
        name="rim",
    )(*sources)
    halo = lax.ppermute(rims, "ctx", [(i, (i + 1) % ranks) for i in range(ranks)])

    lead_shape = jax.ShapeDtypeStruct((length, 2 * width), BF16)
    tail_shape = jax.ShapeDtypeStruct((width, 2 * LANES), BF16)
    scan_shape = lambda count: jax.ShapeDtypeStruct((count, modes, width), F32)
    row_shape = jax.ShapeDtypeStruct((modes, width), F32)
    lead, tail, row, plain, hop, seam, span, reach = pl.pallas_call(
        functools.partial(table_kernel, ranks),
        in_specs=[VMEM] * 3,
        out_specs=[VMEM] * 8,
        out_shape=[
            lead_shape,
            tail_shape,
            jax.ShapeDtypeStruct((2, width), F32),
            jax.ShapeDtypeStruct((1, width), F32),
            row_shape,
            scan_shape(2),
            scan_shape(max(1, spans)),
            scan_shape(reaches),
        ],
        compiler_params=PARAMS,
        cost_estimate=pl.CostEstimate(flops=10**7, bytes_accessed=5 << 20, transcendentals=0),
        name="tables",
    )(residues, decay_rate, skip_gain)

    tile = min(width, WIDE)
    cols = lambda rows: pl.BlockSpec((rows, tile), lambda j: (0, j))
    gated_shape = jax.ShapeDtypeStruct((length, width), F32)
    enter_shape = scan_shape(length // LANES - 1)
    gated, fresh, enter = pl.pallas_call(
        functools.partial(state_kernel, size),
        grid=(width // tile,),
        in_specs=[
            cols(length),
            cols(length),
            pl.BlockSpec((3, 3, tile), lambda j: (0, 0, j)),
            VMEM,
            VMEM,
            VMEM,
        ],
        out_specs=[VMEM] * 3,
        out_shape=[gated_shape, row_shape, enter_shape],
        scratch_shapes=[pltpu.VMEM((SUB + length, LANES), F32)] * 2,
        compiler_params=PARAMS,
        cost_estimate=pl.CostEstimate(flops=10**7, bytes_accessed=5 << 20, transcendentals=0),
        name="state",
    )(key_in, value_in, short_filter, tail, hop, query_in)
    fresh, into, gated = pl.pallas_call(
        seam_kernel,
        in_specs=[VMEM] * 9,
        out_specs=[VMEM] * 3,
        out_shape=[row_shape, enter_shape, gated_shape],
        input_output_aliases={8: 2},
        scratch_shapes=[pltpu.VMEM((2 * SUB, width), F32)] * 2,
        compiler_params=PARAMS,
        name="seam",
    )(halo, key_in, value_in, short_filter, seam, hop, fresh, enter, gated)

    query = pl.pallas_call(
        query_kernel,
        in_specs=[VMEM] * 3,
        out_specs=VMEM,
        out_shape=gated_shape,
        scratch_shapes=[pltpu.VMEM((SUB + length, LANES), F32)],
        compiler_params=PARAMS,
        cost_estimate=pl.CostEstimate(flops=10**7, bytes_accessed=4 << 20, transcendentals=0),
        name="query",
    )(halo, query_in, short_filter)

    cuts = [width // LANES * b // len(steps) * LANES for b in range(len(steps) + 1)]
    nears, total, prefix, first, at = [], fresh, [], 0, 0
    for b, (low, count) in enumerate(steps):
        gots = []
        for m in range(1, 1 << count):
            gots.append(lax.ppermute(total, "ctx", [(i, i ^ (m << low)) for i in range(ranks)]))
        lanes = cuts[b + 1] - cuts[b]
        if lanes:
            nears.append(
                pl.pallas_call(
                    functools.partial(near_kernel, size, cuts[b]),
                    in_specs=[VMEM] * 6,
                    out_specs=VMEM,
                    out_shape=jax.ShapeDtypeStruct((length, lanes), F32),
                    compiler_params=PARAMS,
                    cost_estimate=pl.CostEstimate(flops=10**7, bytes_accessed=4 << 20, transcendentals=0),
                    name="near",
                )(gated, query, into, row, plain, lead)
            )
        if b + 1 < len(steps):
            total, ahead = pl.pallas_call(
                functools.partial(merge_kernel, first, at),
                in_specs=[VMEM] * (3 + len(gots) + len(prefix)),
                out_specs=[VMEM] * 2,
                out_shape=[row_shape] * 2,
                compiler_params=PARAMS,
                name="merge",
            )(total, *gots, *prefix, span, reach)
            prefix = [ahead]
            first += len(gots)
            at += 1 << count

    return pl.pallas_call(
        functools.partial(mix_kernel, size, first, len(gots), len(nears)),
        in_specs=[VMEM] * (3 + len(gots) + len(nears) + len(prefix)),
        out_specs=pl.BlockSpec(memory_space=pl.ANY),
        out_shape=jax.ShapeDtypeStruct((length, width), BF16),
        scratch_shapes=[
            pltpu.VMEM((length, width), BF16),
            pltpu.SemaphoreType.DMA((width // LANES,)),
        ],
        compiler_params=PARAMS,
        name="mix",
    )(query, reach, lead, *gots, *nears, *prefix)


def solution(mesh):
    placed = (
        P("ctx", "fsdp"),
        P("ctx", "fsdp"),
        P("ctx", "fsdp"),
        P(None, "fsdp"),
        P(None, "fsdp"),
        P(None, None, "fsdp"),
        P(None, "fsdp"),
    )
    return jax.shard_map(body, mesh=mesh, in_specs=placed, out_specs=P("ctx", "fsdp"), check_vma=False)
```

```python
import functools

import jax
import jax.numpy as jnp
from jax import lax
from jax.experimental import pallas as pl
from jax.experimental.pallas import tpu as pltpu
from jax.sharding import PartitionSpec as P


LANES = 128
SUB = 8
F32 = jnp.float32
BF16 = jnp.bfloat16
VMEM = pl.BlockSpec(memory_space=pltpu.VMEM)
PARAMS = pltpu.CompilerParams(vmem_limit_bytes=8 << 20)


def split2(x):
    hi = x.astype(BF16)
    return hi, (x - hi.astype(F32)).astype(BF16)


def pair(hi, lo):
    return jnp.concatenate([jnp.concatenate([hi, lo], 1), jnp.concatenate([hi, jnp.zeros_like(lo)], 1)], 0)


def dot3(left, right):
    out = jnp.dot(left, right, preferred_element_type=F32)
    return out[:, :LANES] + out[:, LANES:]


def expand(table, first, lanes, size):
    groups = table.shape[1]
    row = lax.broadcasted_iota(jnp.int32, (groups, lanes), 0)
    col = lax.broadcasted_iota(jnp.int32, (groups, lanes), 1)
    pick = (row == first + col // size).astype(BF16)
    one, _ = split2(table)
    two, three = split2(table - one.astype(F32))
    out = jnp.dot(one, pick, preferred_element_type=F32)
    out = out + jnp.dot(two, pick, preferred_element_type=F32)
    return out + jnp.dot(three, pick, preferred_element_type=F32)


def norm_of(decay):
    x = 2.0 * decay
    total = jnp.full_like(x, 1.0)
    for k in range(9, 1, -1):
        total = 1.0 - x * total * (1.0 / k)
    return jnp.sqrt(x * total)


def short3(ref, start, count, taps):
    at = SUB + start
    out = taps[0] * ref[at : at + count]
    out = out + taps[1] * ref[at - 1 : at - 1 + count]
    return out + taps[2] * ref[at - 2 : at - 2 + count]


def rim_kernel(q_ref, k_ref, v_ref, *refs):
    small, out_ref, loaded, rows, sem = refs[:3], refs[3], refs[4:7], refs[7], refs[8]
    pairs = [(ref.at[ref.shape[0] - SUB :], rows.at[i]) for i, ref in enumerate((q_ref, k_ref, v_ref))]
    pairs += list(zip(small, loaded))
    copies = [pltpu.make_async_copy(src, dst, sem.at[i]) for i, (src, dst) in enumerate(pairs)]
    for copy in copies:
        copy.start()
    for copy in copies:
        copy.wait()
    ends = [rows[i].astype(F32)[SUB - 2 :] for i in range(3)]
    out_ref[...] = jnp.concatenate(ends + ends[:1], 0).astype(BF16)


def past(halo_ref, which, at=slice(None)):
    keep = jnp.where(lax.axis_index("ctx") > 0, 1.0, 0.0).astype(F32)
    return halo_ref[:, at].astype(F32)[2 * which : 2 * which + 2] * keep


def steps_of(ranks):
    bits = ranks.bit_length() - 1
    return [(low, min(2, bits - low)) for low in range(0, bits, 2)]


def gaps_of(ranks, length):
    me = lax.axis_index("ctx")
    table = []
    for low, count in steps_of(ranks):
        mine = (me >> low) % (1 << count)
        inner = me % (1 << low) * length
        size = length << low
        row = []
        for m in range(1 << count):
            other = mine ^ m
            reach = size * (mine - 1 - other) + inner
            after = size * ((1 << count) - 1 - other)
            row.append((other < mine, jnp.maximum(reach, 0).astype(F32), after.astype(F32)))
        table.append(row)
    return table


def table_kernel(res_ref, decay_ref, skip_ref, tail_ref, row_ref, plain_ref, rate_ref, hop_ref, seam_ref):
    modes, width = hop_ref.shape
    plain_ref[...] = skip_ref[...]
    lane = lax.broadcasted_iota(jnp.int32, (modes, LANES), 1)
    own = lane % modes == lax.broadcasted_iota(jnp.int32, (modes, LANES), 0)
    along = lax.broadcasted_iota(jnp.int32, (LANES, LANES), 1).astype(F32)
    for tile in range(width // LANES):
        at = slice(tile * LANES, (tile + 1) * LANES)
        rates = expand(decay_ref[...], tile * (LANES // modes), LANES, modes)
        gains = expand(res_ref[...], tile * (LANES // modes), LANES, modes) * norm_of(rates)
        rate = jnp.sum(jnp.where(own, rates, 0.0), axis=0, keepdims=True)
        row_ref[0:1, at] = rate
        row_ref[1:2, at] = jnp.sum(jnp.where(own, gains, 0.0), axis=0, keepdims=True)
        rate_ref[:, at] = rates
        hop_ref[:, at] = jnp.exp(-rates * float(LANES))
        for i in range(2):
            seam_ref[i, :, at] = jnp.exp(-rates * (LANES - 1.0 - i))
        rate_rows = jnp.transpose(jnp.broadcast_to(rate, (LANES, LANES)))
        tail_ref[at, 0:LANES], tail_ref[at, LANES:] = split2(jnp.exp(-rate_rows * (LANES - 1.0 - along)))


def lead_kernel(ranks, row_ref, rate_ref, lead_ref, span_ref, reach_ref):
    length, width = lead_ref.shape[0], rate_ref.shape[1]
    gaps = gaps_of(ranks, length)
    down = lax.broadcasted_iota(jnp.int32, (LANES, LANES), 0).astype(F32)
    for tile in range(width // LANES):
        at = slice(tile * LANES, (tile + 1) * LANES)
        rates = rate_ref[:, at]
        e = f = 0
        for step, row in enumerate(gaps):
            for m, (before, gap, after) in enumerate(row):
                if m:
                    reach_ref[e, :, at] = jnp.where(before, jnp.exp(-rates * gap), 0.0)
                    e += 1
                if step + 1 < len(gaps):
                    span_ref[f, :, at] = jnp.exp(-rates * after)
                    f += 1
        rate = row_ref[0:1, at]
        lead = row_ref[1:2, at] * jnp.exp(-rate * (down + 1.0))
        hop = jnp.exp(-rate * float(LANES))
        mid = 2 * tile * LANES + LANES
        for c in range(length // LANES):
            rows = slice(c * LANES, (c + 1) * LANES)
            lead_ref[rows, mid - LANES : mid], lead_ref[rows, mid : mid + LANES] = split2(lead)
            lead = lead * hop


def state_kernel(size, k_ref, v_ref, sf_ref, tail_ref, hop_ref, q_ref, gated_ref, fresh_ref, enter_ref, kfs, vfs):
    length, width = k_ref.shape
    modes = fresh_ref.shape[0]
    row = lax.broadcasted_iota(jnp.int32, (modes, LANES), 1) // size
    piece = 64
    inner = lax.broadcasted_iota(jnp.int32, (piece, LANES), 0) >= 2
    for slot in range(2):
        kfs[slot, 0:SUB] = jnp.zeros((SUB, LANES), F32)
        vfs[slot, 0:SUB] = jnp.zeros((SUB, LANES), F32)

    def two(i, carry):
        for slot in range(2):
            one(pl.multiple_of((2 * i + slot) * LANES, LANES), slot)
        return carry

    def one(base, slot):
        at = pl.ds(base, LANES)
        kf, vf = kfs.at[slot], vfs.at[slot]
        kt = [sf_ref[1, i : i + 1, at] for i in range(3)]
        vt = [sf_ref[2, i : i + 1, at] for i in range(3)]
        hop = hop_ref[:, at]
        tail = tail_ref[at, :]
        total = jnp.zeros((modes, LANES), F32)
        for c in range(length // LANES):
            his, los = [], []
            for start in range(c * LANES, (c + 1) * LANES, piece):
                rows = slice(start, start + piece)
                kf[SUB + start : SUB + start + piece] = k_ref[rows, at].astype(F32)
                vf[SUB + start : SUB + start + piece] = v_ref[rows, at].astype(F32)
                gated = short3(kf, start, piece, kt) * short3(vf, start, piece, vt)
                if start == 0:
                    gated = jnp.where(inner, gated, 0.0)
                gated_ref[rows, at] = gated
                hi, lo = split2(gated)
                his.append(hi)
                los.append(lo)
            out = dot3(tail, pair(jnp.concatenate(his, 0), jnp.concatenate(los, 0)))
            fresh = jnp.zeros((modes, LANES), F32)
            for g in range(LANES // size):
                fresh = jnp.where(row == g, out[g * modes : (g + 1) * modes], fresh)
            if c:
                enter_ref[c - 1, :, at] = total
            total = total * hop + fresh
        fresh_ref[:, at] = total

    lax.fori_loop(0, width // (2 * LANES), two, 0)


def seam_kernel(halo_ref, k_ref, v_ref, sf_ref, seam_ref, hop_ref, fresh_ref, enter_ref, gated_ref, out_ref, into_ref, whole_ref, kf, vf):
    kf[SUB - 2 : SUB] = past(halo_ref, 1)
    vf[SUB - 2 : SUB] = past(halo_ref, 2)
    kf[SUB:] = k_ref[0:SUB].astype(F32)
    vf[SUB:] = v_ref[0:SUB].astype(F32)
    kt = [sf_ref[1, i : i + 1, :] for i in range(3)]
    vt = [sf_ref[2, i : i + 1, :] for i in range(3)]
    head = short3(kf, 0, SUB, kt) * short3(vf, 0, SUB, vt)
    whole_ref[0:SUB] = head
    first = seam_ref[0] * head[0:1] + seam_ref[1] * head[1:2]
    for c in range(enter_ref.shape[0]):
        into_ref[c] = enter_ref[c] + first
        first = first * hop_ref[...]
    out_ref[...] = fresh_ref[...] + first


def merge_kernel(first, at, *refs):
    span_ref, reach_ref, total_ref, next_ref = refs[-4:]
    got = refs[1 : -4 if first == 0 else -5]
    total = span_ref[at] * refs[0][...]
    prefix = 0.0 if first == 0 else refs[-5][...]
    for m, ref in enumerate(got):
        value = ref[...]
        total = total + span_ref[at + 1 + m] * value
        prefix = prefix + reach_ref[first + m] * value
    total_ref[...] = total
    next_ref[...] = prefix


def query_kernel(halo_ref, q_ref, sf_ref, out_ref, qf):
    length, width = q_ref.shape
    for lane in range(0, width, LANES):
        at = slice(lane, lane + LANES)
        taps = [sf_ref[0, i : i + 1, at] for i in range(3)]
        qf[SUB - 2 : SUB] = past(halo_ref, 0, at)
        piece = 64
        for start in range(0, length, piece):
            rows = slice(start, start + piece)
            qf[SUB + start : SUB + start + piece] = q_ref[rows, at].astype(F32)
            out_ref[rows, at] = short3(qf, start, piece, taps)


def near_kernel(size, first, gated_ref, into_ref, row_ref, plain_ref, lead_ref, out_ref):
    length, lanes = out_ref.shape
    modes = into_ref.shape[1]
    chunks = length // LANES
    groups = LANES // size
    down = lax.broadcasted_iota(jnp.int32, (LANES, LANES), 0)
    along = lax.broadcasted_iota(jnp.int32, (LANES, LANES), 1)
    causal = along >= down
    block = down // modes == along // size

    for tile in range(lanes // LANES):
        at = slice(first + tile * LANES, first + (tile + 1) * LANES)
        to = slice(tile * LANES, (tile + 1) * LANES)
        rate = jnp.transpose(jnp.broadcast_to(row_ref[0:1, at], (LANES, LANES)))
        gain = jnp.transpose(jnp.broadcast_to(row_ref[1:2, at], (LANES, LANES)))
        curve = gain * jnp.exp(-rate * along.astype(F32))
        halves = [split2(jnp.transpose(gated_ref[c * LANES : (c + 1) * LANES, at])) for c in range(chunks)]
        outs = []
        for g in range(groups):
            rows = slice(g * size, (g + 1) * size)
            taps = jnp.sum(curve[g * modes : (g + 1) * modes], axis=0, keepdims=True)
            toe = pltpu.roll(jnp.broadcast_to(taps, (LANES, LANES)), 0, 1, stride=1, stride_axis=0)
            hi, lo = split2(jnp.where(causal, toe, 0.0))
            xh = jnp.concatenate([h[rows] for h, _ in halves], 0)
            xl = jnp.concatenate([l[rows] for _, l in halves], 0)
            outs.append(dot3(jnp.concatenate([xh, xl], 1), pair(hi, lo)))
        lead = lead_ref[0:LANES, 2 * at.start : 2 * at.stop]
        for c in range(chunks):
            rows = slice(c * LANES, (c + 1) * LANES)
            near = jnp.transpose(jnp.concatenate([o[c * size : (c + 1) * size] for o in outs], 0))
            near = near + plain_ref[:, at] * gated_ref[rows, at]
            if c:
                wide = jnp.where(block, jnp.concatenate([into_ref[c - 1, :, at]] * groups, 0), 0.0)
                near = near + dot3(lead, pair(*split2(wide)))
            out_ref[rows, to] = near


def mix_kernel(size, first, count, parts, *refs):
    query_ref, reach_ref, lead_ref = refs[:3]
    gots = refs[3 : 3 + count]
    nears = refs[3 + count : 3 + count + parts]
    prefix = refs[3 + count + parts : -3]
    out_ref, stage, sem = refs[-3:]
    length, width = query_ref.shape
    modes = reach_ref.shape[1]
    where = []
    for ref in nears:
        where += [(ref, c) for c in range(0, ref.shape[1], LANES)]
    groups = LANES // size
    row = lax.broadcasted_iota(jnp.int32, (groups * modes, LANES), 0)
    col = lax.broadcasted_iota(jnp.int32, (groups * modes, LANES), 1)
    block = row // modes == col // size
    copies = []
    for tile in range(width // LANES):
        at = slice(tile * LANES, (tile + 1) * LANES)
        state = prefix[0][:, at] if prefix else 0.0
        for m in range(count):
            state = state + reach_ref[first + m, :, at] * gots[m][:, at]
        wide = jnp.where(block, jnp.concatenate([state] * groups, 0), 0.0)
        right = pair(*split2(wide))
        near, c = where[tile]
        for start in range(0, length, LANES):
            rows = slice(start, start + LANES)
            term = dot3(lead_ref[rows, 2 * at.start : 2 * at.stop], right)
            stage[rows, at] = (query_ref[rows, at] * (near[rows, c : c + LANES] + term)).astype(BF16)
        copy = pltpu.make_async_copy(stage.at[:, at], out_ref.at[:, at], sem.at[tile])
        copy.start()
        copies.append(copy)
    for copy in copies:
        copy.wait()


def body(query_in, key_in, value_in, residues, decay_rate, short_filter, skip_gain):
    length, width = query_in.shape
    modes, groups = residues.shape
    size = width // groups
    ranks = lax.axis_size("ctx")
    steps = steps_of(ranks)
    reaches = sum((1 << count) - 1 for _, count in steps)
    spans = sum(1 << count for _, count in steps[:-1])
    small = (residues, decay_rate, skip_gain)
    sources = [pltpu.with_memory_space_constraint(a, pltpu.HBM) for a in (query_in, key_in, value_in) + small]
    rims, residues, decay_rate, skip_gain = pl.pallas_call(
        rim_kernel,
        in_specs=[pl.BlockSpec(memory_space=pltpu.HBM)] * 6,
        out_specs=[VMEM] * 4,
        out_shape=[jax.ShapeDtypeStruct((SUB, width), BF16)] + [jax.ShapeDtypeStruct(a.shape, F32) for a in small],
        scratch_shapes=[pltpu.VMEM((3, SUB, width), BF16), pltpu.SemaphoreType.DMA((6,))],
        compiler_params=PARAMS,
        name="rim",
    )(*sources)
    halo = lax.ppermute(rims, "ctx", [(i, (i + 1) % ranks) for i in range(ranks)])

    lead_shape = jax.ShapeDtypeStruct((length, 2 * width), BF16)
    tail_shape = jax.ShapeDtypeStruct((width, 2 * LANES), BF16)
    scan_shape = lambda count: jax.ShapeDtypeStruct((count, modes, width), F32)
    row_shape = jax.ShapeDtypeStruct((modes, width), F32)
    tail, row, plain, rate, hop, seam = pl.pallas_call(
        table_kernel,
        in_specs=[VMEM] * 3,
        out_specs=[VMEM] * 6,
        out_shape=[
            tail_shape,
            jax.ShapeDtypeStruct((2, width), F32),
            jax.ShapeDtypeStruct((1, width), F32),
            row_shape,
            row_shape,
            scan_shape(2),
        ],
        compiler_params=PARAMS,
        cost_estimate=pl.CostEstimate(flops=10**7, bytes_accessed=5 << 20, transcendentals=0),
        name="tables",
    )(residues, decay_rate, skip_gain)
    lead, span, reach = pl.pallas_call(
        functools.partial(lead_kernel, ranks),
        in_specs=[VMEM] * 2,
        out_specs=[VMEM] * 3,
        out_shape=[lead_shape, scan_shape(max(1, spans)), scan_shape(reaches)],
        compiler_params=PARAMS,
        cost_estimate=pl.CostEstimate(flops=10**7, bytes_accessed=2 << 20, transcendentals=0),
        name="lead",
    )(row, rate)

    gated_shape = jax.ShapeDtypeStruct((length, width), F32)
    enter_shape = scan_shape(length // LANES - 1)
    gated, fresh, enter = pl.pallas_call(
        functools.partial(state_kernel, size),
        in_specs=[VMEM] * 6,
        out_specs=[VMEM] * 3,
        out_shape=[gated_shape, row_shape, enter_shape],
        scratch_shapes=[pltpu.VMEM((2, SUB + length, LANES), F32)] * 2,
        compiler_params=PARAMS,
        cost_estimate=pl.CostEstimate(flops=10**7, bytes_accessed=5 << 20, transcendentals=0),
        name="state",
    )(key_in, value_in, short_filter, tail, hop, query_in)
    fresh, into, gated = pl.pallas_call(
        seam_kernel,
        in_specs=[VMEM] * 9,
        out_specs=[VMEM] * 3,
        out_shape=[row_shape, enter_shape, gated_shape],
        input_output_aliases={8: 2},
        scratch_shapes=[pltpu.VMEM((2 * SUB, width), F32)] * 2,
        compiler_params=PARAMS,
        name="seam",
    )(halo, key_in, value_in, short_filter, seam, hop, fresh, enter, gated)

    query = pl.pallas_call(
        query_kernel,
        in_specs=[VMEM] * 3,
        out_specs=VMEM,
        out_shape=gated_shape,
        scratch_shapes=[pltpu.VMEM((SUB + length, LANES), F32)],
        compiler_params=PARAMS,
        cost_estimate=pl.CostEstimate(flops=10**7, bytes_accessed=4 << 20, transcendentals=0),
        name="query",
    )(halo, query_in, short_filter)

    tiles = width // LANES
    head = tiles * 4 // 8
    cuts = [0] + [(head + (tiles - head) * b // max(1, len(steps) - 1)) * LANES for b in range(len(steps))]
    nears, total, prefix, first, at = [], fresh, [], 0, 0
    for b, (low, count) in enumerate(steps):
        gots = []
        for m in range(1, 1 << count):
            gots.append(lax.ppermute(total, "ctx", [(i, i ^ (m << low)) for i in range(ranks)]))
        lanes = cuts[b + 1] - cuts[b]
        if lanes:
            nears.append(
                pl.pallas_call(
                    functools.partial(near_kernel, size, cuts[b]),
                    in_specs=[VMEM] * 5,
                    out_specs=VMEM,
                    out_shape=jax.ShapeDtypeStruct((length, lanes), F32),
                    compiler_params=PARAMS,
                    cost_estimate=pl.CostEstimate(flops=10**7, bytes_accessed=4 << 20, transcendentals=0),
                    name="near",
                )(gated, into, row, plain, lead)
            )
        if b + 1 < len(steps):
            total, ahead = pl.pallas_call(
                functools.partial(merge_kernel, first, at),
                in_specs=[VMEM] * (3 + len(gots) + len(prefix)),
                out_specs=[VMEM] * 2,
                out_shape=[row_shape] * 2,
                compiler_params=PARAMS,
                name="merge",
            )(total, *gots, *prefix, span, reach)
            prefix = [ahead]
            first += len(gots)
            at += 1 << count

    return pl.pallas_call(
        functools.partial(mix_kernel, size, first, len(gots), len(nears)),
        in_specs=[VMEM] * (3 + len(gots) + len(nears) + len(prefix)),
        out_specs=pl.BlockSpec(memory_space=pl.ANY),
        out_shape=jax.ShapeDtypeStruct((length, width), BF16),
        scratch_shapes=[
            pltpu.VMEM((length, width), BF16),
            pltpu.SemaphoreType.DMA((width // LANES,)),
        ],
        compiler_params=PARAMS,
        name="mix",
    )(query, reach, lead, *gots, *nears, *prefix)


def solution(mesh):
    placed = (
        P("ctx", "fsdp"),
        P("ctx", "fsdp"),
        P("ctx", "fsdp"),
        P(None, "fsdp"),
        P(None, "fsdp"),
        P(None, None, "fsdp"),
        P(None, "fsdp"),
    )
    return jax.shard_map(body, mesh=mesh, in_specs=placed, out_specs=P("ctx", "fsdp"), check_vma=False)
```

```python
import functools

import jax
import jax.numpy as jnp
from jax import lax
from jax.experimental import pallas as pl
from jax.experimental.pallas import tpu as pltpu
from jax.sharding import PartitionSpec as P


LANES = 128
SUB = 8
F32 = jnp.float32
BF16 = jnp.bfloat16
VMEM = pl.BlockSpec(memory_space=pltpu.VMEM)
PARAMS = pltpu.CompilerParams(vmem_limit_bytes=8 << 20)
PACKED = pltpu.CompilerParams(vmem_limit_bytes=8 << 20)


def split2(x):
    hi = x.astype(BF16)
    return hi, (x - hi.astype(F32)).astype(BF16)


def pair(hi, lo):
    return jnp.concatenate([jnp.concatenate([hi, lo], 1), jnp.concatenate([hi, jnp.zeros_like(lo)], 1)], 0)


def dot3(left, right):
    out = jnp.dot(left, right, preferred_element_type=F32)
    return out[:, :LANES] + out[:, LANES:]


def expand(table, first, lanes, size):
    groups = table.shape[1]
    row = lax.broadcasted_iota(jnp.int32, (groups, lanes), 0)
    col = lax.broadcasted_iota(jnp.int32, (groups, lanes), 1)
    pick = (row == first + col // size).astype(BF16)
    one, _ = split2(table)
    two, three = split2(table - one.astype(F32))
    out = jnp.dot(one, pick, preferred_element_type=F32)
    out = out + jnp.dot(two, pick, preferred_element_type=F32)
    return out + jnp.dot(three, pick, preferred_element_type=F32)


def norm_of(decay):
    x = 2.0 * decay
    total = jnp.full_like(x, 1.0)
    for k in range(9, 1, -1):
        total = 1.0 - x * total * (1.0 / k)
    return jnp.sqrt(x * total)


def short3(ref, start, count, taps):
    at = SUB + start
    out = taps[0] * ref[at : at + count]
    out = out + taps[1] * ref[at - 1 : at - 1 + count]
    return out + taps[2] * ref[at - 2 : at - 2 + count]


def rim_kernel(q_ref, k_ref, v_ref, *refs):
    small, out_ref, loaded, rows, sem = refs[:3], refs[3], refs[4:7], refs[7], refs[8]
    pairs = [(ref.at[ref.shape[0] - SUB :], rows.at[i]) for i, ref in enumerate((q_ref, k_ref, v_ref))]
    pairs += list(zip(small, loaded))
    copies = [pltpu.make_async_copy(src, dst, sem.at[i]) for i, (src, dst) in enumerate(pairs)]
    for copy in copies:
        copy.start()
    for copy in copies:
        copy.wait()
    ends = [rows[i].astype(F32)[SUB - 2 :] for i in range(3)]
    out_ref[...] = jnp.concatenate(ends + ends[:1], 0).astype(BF16)


def past(halo_ref, which, at=slice(None)):
    keep = jnp.where(lax.axis_index("ctx") > 0, 1.0, 0.0).astype(F32)
    return halo_ref[:, at].astype(F32)[2 * which : 2 * which + 2] * keep


def steps_of(ranks):
    bits = ranks.bit_length() - 1
    return [(low, min(2, bits - low)) for low in range(0, bits, 2)]


def gaps_of(ranks, length):
    me = lax.axis_index("ctx")
    table = []
    for low, count in steps_of(ranks):
        mine = (me >> low) % (1 << count)
        inner = me % (1 << low) * length
        size = length << low
        row = []
        for m in range(1 << count):
            other = mine ^ m
            reach = size * (mine - 1 - other) + inner
            after = size * ((1 << count) - 1 - other)
            row.append((other < mine, jnp.maximum(reach, 0).astype(F32), after.astype(F32)))
        table.append(row)
    return table


def table_kernel(ranks, res_ref, decay_ref, skip_ref, lead_ref, tail_ref, row_ref, plain_ref, hop_ref, seam_ref, span_ref, reach_ref):
    length, width = lead_ref.shape[0], skip_ref.shape[1]
    modes = decay_ref.shape[0]
    gaps = gaps_of(ranks, length)
    plain_ref[...] = skip_ref[...]
    lane = lax.broadcasted_iota(jnp.int32, (modes, LANES), 1)
    own = lane % modes == lax.broadcasted_iota(jnp.int32, (modes, LANES), 0)
    down = lax.broadcasted_iota(jnp.int32, (LANES, LANES), 0).astype(F32)
    along = lax.broadcasted_iota(jnp.int32, (LANES, LANES), 1).astype(F32)
    for tile in range(width // LANES):
        at = slice(tile * LANES, (tile + 1) * LANES)
        rates = expand(decay_ref[...], tile * (LANES // modes), LANES, modes)
        gains = expand(res_ref[...], tile * (LANES // modes), LANES, modes) * norm_of(rates)
        rate = jnp.sum(jnp.where(own, rates, 0.0), axis=0, keepdims=True)
        gain = jnp.sum(jnp.where(own, gains, 0.0), axis=0, keepdims=True)
        row_ref[0:1, at] = rate
        row_ref[1:2, at] = gain
        hop_ref[:, at] = jnp.exp(-rates * float(LANES))
        for i in range(2):
            seam_ref[i, :, at] = jnp.exp(-rates * (LANES - 1.0 - i))
        e = f = 0
        for step, row in enumerate(gaps):
            for m, (before, gap, after) in enumerate(row):
                if m:
                    reach_ref[e, :, at] = jnp.where(before, jnp.exp(-rates * gap), 0.0)
                    e += 1
                if step + 1 < len(gaps):
                    span_ref[f, :, at] = jnp.exp(-rates * after)
                    f += 1
        rate_rows = jnp.transpose(jnp.broadcast_to(rate, (LANES, LANES)))
        tail_ref[at, 0:LANES], tail_ref[at, LANES:] = split2(jnp.exp(-rate_rows * (LANES - 1.0 - along)))
        lead = gain * jnp.exp(-rate * (down + 1.0))
        hop = jnp.exp(-rate * float(LANES))
        for c in range(length // LANES):
            rows = slice(c * LANES, (c + 1) * LANES)
            mid = 2 * tile * LANES + LANES
            lead_ref[rows, mid - LANES : mid], lead_ref[rows, mid : mid + LANES] = split2(lead)
            lead = lead * hop


def state_kernel(size, k_ref, v_ref, sf_ref, tail_ref, hop_ref, q_ref, gated_ref, fresh_ref, enter_ref, kfs, vfs):
    length, width = k_ref.shape
    modes = fresh_ref.shape[0]
    row = lax.broadcasted_iota(jnp.int32, (modes, LANES), 1) // size
    piece = 64
    inner = lax.broadcasted_iota(jnp.int32, (piece, LANES), 0) >= 2
    for slot in range(2):
        kfs[slot, 0:SUB] = jnp.zeros((SUB, LANES), F32)
        vfs[slot, 0:SUB] = jnp.zeros((SUB, LANES), F32)

    def two(i, carry):
        for slot in range(2):
            one(pl.multiple_of((2 * i + slot) * LANES, LANES), slot)
        return carry

    def one(base, slot):
        at = pl.ds(base, LANES)
        kf, vf = kfs.at[slot], vfs.at[slot]
        kt = [sf_ref[1, i : i + 1, at] for i in range(3)]
        vt = [sf_ref[2, i : i + 1, at] for i in range(3)]
        hop = hop_ref[:, at]
        tail = tail_ref[at, :]
        total = jnp.zeros((modes, LANES), F32)
        for c in range(length // LANES):
            his, los = [], []
            for start in range(c * LANES, (c + 1) * LANES, piece):
                rows = slice(start, start + piece)
                kf[SUB + start : SUB + start + piece] = k_ref[rows, at].astype(F32)
                vf[SUB + start : SUB + start + piece] = v_ref[rows, at].astype(F32)
                gated = short3(kf, start, piece, kt) * short3(vf, start, piece, vt)
                if start == 0:
                    gated = jnp.where(inner, gated, 0.0)
                gated_ref[rows, at] = gated
                hi, lo = split2(gated)
                his.append(hi)
                los.append(lo)
            out = dot3(tail, pair(jnp.concatenate(his, 0), jnp.concatenate(los, 0)))
            fresh = jnp.zeros((modes, LANES), F32)
            for g in range(LANES // size):
                fresh = jnp.where(row == g, out[g * modes : (g + 1) * modes], fresh)
            if c:
                enter_ref[c - 1, :, at] = total
            total = total * hop + fresh
        fresh_ref[:, at] = total

    lax.fori_loop(0, width // (2 * LANES), two, 0)


def seam_kernel(halo_ref, k_ref, v_ref, sf_ref, seam_ref, hop_ref, fresh_ref, enter_ref, gated_ref, out_ref, into_ref, whole_ref, kf, vf):
    kf[SUB - 2 : SUB] = past(halo_ref, 1)
    vf[SUB - 2 : SUB] = past(halo_ref, 2)
    kf[SUB:] = k_ref[0:SUB].astype(F32)
    vf[SUB:] = v_ref[0:SUB].astype(F32)
    kt = [sf_ref[1, i : i + 1, :] for i in range(3)]
    vt = [sf_ref[2, i : i + 1, :] for i in range(3)]
    head = short3(kf, 0, SUB, kt) * short3(vf, 0, SUB, vt)
    whole_ref[0:SUB] = head
    first = seam_ref[0] * head[0:1] + seam_ref[1] * head[1:2]
    for c in range(enter_ref.shape[0]):
        into_ref[c] = enter_ref[c] + first
        first = first * hop_ref[...]
    out_ref[...] = fresh_ref[...] + first


def merge_kernel(first, at, *refs):
    span_ref, reach_ref, total_ref, next_ref = refs[-4:]
    got = refs[1 : -4 if first == 0 else -5]
    total = span_ref[at] * refs[0][...]
    prefix = 0.0 if first == 0 else refs[-5][...]
    for m, ref in enumerate(got):
        value = ref[...]
        total = total + span_ref[at + 1 + m] * value
        prefix = prefix + reach_ref[first + m] * value
    total_ref[...] = total
    next_ref[...] = prefix


def query_kernel(halo_ref, q_ref, sf_ref, out_ref, qf):
    length, width = q_ref.shape
    for lane in range(0, width, LANES):
        at = slice(lane, lane + LANES)
        taps = [sf_ref[0, i : i + 1, at] for i in range(3)]
        qf[SUB - 2 : SUB] = past(halo_ref, 0, at)
        piece = 64
        for start in range(0, length, piece):
            rows = slice(start, start + piece)
            qf[SUB + start : SUB + start + piece] = q_ref[rows, at].astype(F32)
            out_ref[rows, at] = short3(qf, start, piece, taps)


def near_kernel(size, first, gated_ref, query_ref, into_ref, row_ref, plain_ref, lead_ref, out_ref):
    length, lanes = out_ref.shape
    modes = into_ref.shape[1]
    chunks = length // LANES
    groups = LANES // size
    down = lax.broadcasted_iota(jnp.int32, (LANES, LANES), 0)
    along = lax.broadcasted_iota(jnp.int32, (LANES, LANES), 1)
    causal = along >= down
    block = down // modes == along // size

    for tile in range(lanes // LANES):
        at = slice(first + tile * LANES, first + (tile + 1) * LANES)
        to = slice(tile * LANES, (tile + 1) * LANES)
        rate = jnp.transpose(jnp.broadcast_to(row_ref[0:1, at], (LANES, LANES)))
        gain = jnp.transpose(jnp.broadcast_to(row_ref[1:2, at], (LANES, LANES)))
        curve = gain * jnp.exp(-rate * along.astype(F32))
        halves = [split2(jnp.transpose(gated_ref[c * LANES : (c + 1) * LANES, at])) for c in range(chunks)]
        outs = []
        for g in range(groups):
            rows = slice(g * size, (g + 1) * size)
            taps = jnp.sum(curve[g * modes : (g + 1) * modes], axis=0, keepdims=True)
            toe = pltpu.roll(jnp.broadcast_to(taps, (LANES, LANES)), 0, 1, stride=1, stride_axis=0)
            hi, lo = split2(jnp.where(causal, toe, 0.0))
            xh = jnp.concatenate([h[rows] for h, _ in halves], 0)
            xl = jnp.concatenate([l[rows] for _, l in halves], 0)
            outs.append(dot3(jnp.concatenate([xh, xl], 1), pair(hi, lo)))
        lead = lead_ref[0:LANES, 2 * at.start : 2 * at.stop]
        for c in range(chunks):
            rows = slice(c * LANES, (c + 1) * LANES)
            near = jnp.transpose(jnp.concatenate([o[c * size : (c + 1) * size] for o in outs], 0))
            near = near + plain_ref[:, at] * gated_ref[rows, at]
            if c:
                wide = jnp.where(block, jnp.concatenate([into_ref[c - 1, :, at]] * groups, 0), 0.0)
                near = near + dot3(lead, pair(*split2(wide)))
            out_ref[rows, to] = query_ref[rows, at] * near


def mix_kernel(size, first, count, parts, *refs):
    query_ref, reach_ref, lead_ref = refs[:3]
    gots = refs[3 : 3 + count]
    nears = refs[3 + count : 3 + count + parts]
    prefix = refs[3 + count + parts : -3]
    out_ref, stage, sem = refs[-3:]
    length, width = query_ref.shape
    modes = reach_ref.shape[1]
    where = []
    for ref in nears:
        where += [(ref, c) for c in range(0, ref.shape[1], LANES)]
    groups = LANES // size
    row = lax.broadcasted_iota(jnp.int32, (groups * modes, LANES), 0)
    col = lax.broadcasted_iota(jnp.int32, (groups * modes, LANES), 1)
    block = row // modes == col // size
    copies = []
    for tile in range(width // LANES):
        at = slice(tile * LANES, (tile + 1) * LANES)
        state = prefix[0][:, at] if prefix else 0.0
        for m in range(count):
            state = state + reach_ref[first + m, :, at] * gots[m][:, at]
        wide = jnp.where(block, jnp.concatenate([state] * groups, 0), 0.0)
        right = pair(*split2(wide))
        near, c = where[tile]
        for start in range(0, length, LANES):
            rows = slice(start, start + LANES)
            term = dot3(lead_ref[rows, 2 * at.start : 2 * at.stop], right)
            stage[rows, at] = (near[rows, c : c + LANES] + query_ref[rows, at] * term).astype(BF16)
        copy = pltpu.make_async_copy(stage.at[:, at], out_ref.at[:, at], sem.at[tile])
        copy.start()
        copies.append(copy)
    for copy in copies:
        copy.wait()


def body(query_in, key_in, value_in, residues, decay_rate, short_filter, skip_gain):
    length, width = query_in.shape
    modes, groups = residues.shape
    size = width // groups
    ranks = lax.axis_size("ctx")
    steps = steps_of(ranks)
    reaches = sum((1 << count) - 1 for _, count in steps)
    spans = sum(1 << count for _, count in steps[:-1])
    small = (residues, decay_rate, skip_gain)
    sources = [pltpu.with_memory_space_constraint(a, pltpu.HBM) for a in (query_in, key_in, value_in) + small]
    rims, residues, decay_rate, skip_gain = pl.pallas_call(
        rim_kernel,
        in_specs=[pl.BlockSpec(memory_space=pltpu.HBM)] * 6,
        out_specs=[VMEM] * 4,
        out_shape=[jax.ShapeDtypeStruct((SUB, width), BF16)] + [jax.ShapeDtypeStruct(a.shape, F32) for a in small],
        scratch_shapes=[pltpu.VMEM((3, SUB, width), BF16), pltpu.SemaphoreType.DMA((6,))],
        compiler_params=PARAMS,
        name="rim",
    )(*sources)
    halo = lax.ppermute(rims, "ctx", [(i, (i + 1) % ranks) for i in range(ranks)])

    lead_shape = jax.ShapeDtypeStruct((length, 2 * width), BF16)
    tail_shape = jax.ShapeDtypeStruct((width, 2 * LANES), BF16)
    scan_shape = lambda count: jax.ShapeDtypeStruct((count, modes, width), F32)
    row_shape = jax.ShapeDtypeStruct((modes, width), F32)
    lead, tail, row, plain, hop, seam, span, reach = pl.pallas_call(
        functools.partial(table_kernel, ranks),
        in_specs=[VMEM] * 3,
        out_specs=[VMEM] * 8,
        out_shape=[
            lead_shape,
            tail_shape,
            jax.ShapeDtypeStruct((2, width), F32),
            jax.ShapeDtypeStruct((1, width), F32),
            row_shape,
            scan_shape(2),
            scan_shape(max(1, spans)),
            scan_shape(reaches),
        ],
        compiler_params=PARAMS,
        cost_estimate=pl.CostEstimate(flops=10**7, bytes_accessed=5 << 20, transcendentals=0),
        name="tables",
    )(residues, decay_rate, skip_gain)

    gated_shape = jax.ShapeDtypeStruct((length, width), F32)
    enter_shape = scan_shape(length // LANES - 1)
    gated, fresh, enter = pl.pallas_call(
        functools.partial(state_kernel, size),
        in_specs=[VMEM] * 6,
        out_specs=[VMEM] * 3,
        out_shape=[gated_shape, row_shape, enter_shape],
        scratch_shapes=[pltpu.VMEM((2, SUB + length, LANES), F32)] * 2,
        compiler_params=PACKED,
        cost_estimate=pl.CostEstimate(flops=10**7, bytes_accessed=5 << 20, transcendentals=0),
        name="state",
    )(key_in, value_in, short_filter, tail, hop, query_in)
    fresh, into, gated = pl.pallas_call(
        seam_kernel,
        in_specs=[VMEM] * 9,
        out_specs=[VMEM] * 3,
        out_shape=[row_shape, enter_shape, gated_shape],
        input_output_aliases={8: 2},
        scratch_shapes=[pltpu.VMEM((2 * SUB, width), F32)] * 2,
        compiler_params=PARAMS,
        name="seam",
    )(halo, key_in, value_in, short_filter, seam, hop, fresh, enter, gated)

    query = pl.pallas_call(
        query_kernel,
        in_specs=[VMEM] * 3,
        out_specs=VMEM,
        out_shape=gated_shape,
        scratch_shapes=[pltpu.VMEM((SUB + length, LANES), F32)],
        compiler_params=PARAMS,
        cost_estimate=pl.CostEstimate(flops=10**7, bytes_accessed=4 << 20, transcendentals=0),
        name="query",
    )(halo, query_in, short_filter)

    cuts = [width // LANES * b // len(steps) * LANES for b in range(len(steps) + 1)]
    nears, total, prefix, first, at = [], fresh, [], 0, 0
    for b, (low, count) in enumerate(steps):
        gots = []
        for m in range(1, 1 << count):
            gots.append(lax.ppermute(total, "ctx", [(i, i ^ (m << low)) for i in range(ranks)]))
        lanes = cuts[b + 1] - cuts[b]
        if lanes:
            nears.append(
                pl.pallas_call(
                    functools.partial(near_kernel, size, cuts[b]),
                    in_specs=[VMEM] * 6,
                    out_specs=VMEM,
                    out_shape=jax.ShapeDtypeStruct((length, lanes), F32),
                    compiler_params=PARAMS,
                    cost_estimate=pl.CostEstimate(flops=10**7, bytes_accessed=4 << 20, transcendentals=0),
                    name="near",
                )(gated, query, into, row, plain, lead)
            )
        if b + 1 < len(steps):
            total, ahead = pl.pallas_call(
                functools.partial(merge_kernel, first, at),
                in_specs=[VMEM] * (3 + len(gots) + len(prefix)),
                out_specs=[VMEM] * 2,
                out_shape=[row_shape] * 2,
                compiler_params=PARAMS,
                name="merge",
            )(total, *gots, *prefix, span, reach)
            prefix = [ahead]
            first += len(gots)
            at += 1 << count

    return pl.pallas_call(
        functools.partial(mix_kernel, size, first, len(gots), len(nears)),
        in_specs=[VMEM] * (3 + len(gots) + len(nears) + len(prefix)),
        out_specs=pl.BlockSpec(memory_space=pl.ANY),
        out_shape=jax.ShapeDtypeStruct((length, width), BF16),
        scratch_shapes=[
            pltpu.VMEM((length, width), BF16),
            pltpu.SemaphoreType.DMA((width // LANES,)),
        ],
        compiler_params=PARAMS,
        name="mix",
    )(query, reach, lead, *gots, *nears, *prefix)


def solution(mesh):
    placed = (
        P("ctx", "fsdp"),
        P("ctx", "fsdp"),
        P("ctx", "fsdp"),
        P(None, "fsdp"),
        P(None, "fsdp"),
        P(None, None, "fsdp"),
        P(None, "fsdp"),
    )
    return jax.shard_map(body, mesh=mesh, in_specs=placed, out_specs=P("ctx", "fsdp"), check_vma=False)
```
